128 devices in a mesh: wide: 32 (over y, z, core), narrow: 4 (over x).
Axes of the slice: x: 4, y: 4, z: 4, core: 2. Of those that a mesh axis runs over, the one named last changes fastest.
Arguments:
- layer_input_rows: bfloat16 [65536, 4096], P('wide', 'narrow'), may hold values from -6 to 6
- output_gradient_rows: bfloat16 [65536, 4096], P('wide', 'narrow'), may hold values from -60 to 60
- adapter_up_weight: bfloat16 [4096, 128], P('narrow'), may hold values from -0.09375 to 0.09375
- input_side_projection: bfloat16 [4096, 128], P('narrow'), may hold values from -0.09375 to 0.09375
- rank_side_projection: bfloat16 [128, 64], replicated, may hold values from -6 to 6
- lengths: int32 [2048], P('wide'), may hold values from 1 to 32, 40960 in all
- program_output_index: int32 [2048], replicated, may hold values from 0 to 2047, each once
- targets: bfloat16 [65536, 8192], P('wide', 'narrow'), may hold values from -650 to 650
Outputs:
- scores: float32 [2048, 65536], P('narrow', 'wide')
The draws below stay inside these ranges and needn't reach their ends.
Inputs may be any that keep to these rules, and one draw needn't show every extreme that they name: Program s uses its first lengths[s] token rows; some program uses all 32. `program_output_index`: each output row is named by exactly one program.
All inputs are finite; a program needn't handle non-finite values. No bound on the sum of `lengths` on one device may be relied on, other than what follows from the above.
Results may differ from the reference program's by a relative error of at most 0.025.
Values may be sent and summed in bfloat16 or wider, within the bound.
A program may use at most 128 MiB of HBM per device.

```python
import math
import jax
import jax.numpy as jnp
import numpy as np
from jax import lax

D = 4096
OUTPUT_WIDTH = 4096
ADAPTER_RANK = 128
K1 = 128
K2 = 64
K = 8192
KPART = 2048
L = 32
TGTB = 2048
S = 2048
TGT = 65536
TOKENS = 65536
N_WIDE = 32
N_NARROW = 4


def column_scales(key, number):
    ramp = jnp.arange(number, dtype=jnp.float32) / max(number - 1, 1)
    rough = jax.random.uniform(key, (number,), jnp.float32)
    return jnp.exp(jnp.log(3.0) * ramp + jnp.log(3.3) * rough)


def draw_rank_side_projection(key, part):
    scales = column_scales(jax.random.fold_in(key, 11), K2)
    base = jax.random.truncated_normal(jax.random.fold_in(key, 12), -6.0, 6.0, (ADAPTER_RANK, K2), jnp.float32)
    return (base * scales[None, :] / math.sqrt(ADAPTER_RANK)).astype(jnp.bfloat16)


def draw_output_gradient_rows(key, part):
    row_scales = jnp.exp(jnp.log(10.0) * jax.random.uniform(jax.random.fold_in(key, 21), (TOKENS, 1), jnp.float32))
    base = jax.random.truncated_normal(jax.random.fold_in(key, 23), -6.0, 6.0, (TOKENS, OUTPUT_WIDTH), jnp.float32)
    return (base * row_scales).astype(jnp.bfloat16)


def draw_targets(key, part):
    scales = jnp.repeat(column_scales(jax.random.fold_in(key, 31), K2), K1)
    row_scales = jnp.exp(jnp.log(10.0) * jax.random.uniform(jax.random.fold_in(key, 32), (TGT, 1), jnp.float32))
    base = jax.random.truncated_normal(jax.random.fold_in(key, 34), -6.0, 6.0, (TGT, K), jnp.float32)
    return (base * scales[None, :] * row_scales).astype(jnp.bfloat16)


def level_of(rng, extent, shards, least, top_value):
    factor_of = 1.0
    for dim, blocks in shards:
        heights = jax.random.uniform(jax.random.fold_in(jax.random.fold_in(rng, 6), dim), (blocks,), jnp.float32, least / len(shards), top_value / len(shards))
        factor_of = factor_of * jnp.repeat(jnp.exp(heights), extent[dim] // blocks).reshape((-1,) + (1,) * (len(extent) - 1 - dim))
    return factor_of


def profile(count, total, most, slope):
    portions = [(1 << 20) // math.isqrt(standing ** slope) + 1 for standing in range(2, count + 1)]
    spare, counts = total - most - (count - 1), [1] * (count - 1)
    while spare > 0:
        candidates = [i for i in range(count - 1) if counts[i] < most]
        mass, remaining = sum([portions[i] for i in candidates]), spare
        for i in candidates:
            addition = min(most - counts[i], max(1, remaining * portions[i] // mass), spare)
            counts[i] = counts[i] + addition
            spare = spare - addition
    return np.array([most] + counts)


def ragged(rng, count, total, most, skew):
    if count == 2:
        one = jax.random.randint(rng, (), max(1, total - most), min(most, total - 1) + 1)
        return jnp.stack([one, total - one])
    sizes = jnp.asarray(profile(count, total, most, skew), jnp.int32)
    pairs = (count - 1) // 2
    giver, taker = sizes[1:1 + 2 * pairs:2], sizes[2:2 + 2 * pairs:2]
    margin = jnp.minimum(giver - 1, most - taker)
    moved = jax.random.randint(jax.random.fold_in(rng, 1), (pairs,), 0, 1 << 20) % (margin + 1)
    sizes = sizes.at[1:1 + 2 * pairs:2].set(giver - moved).at[2:2 + 2 * pairs:2].set(taker + moved)
    return sizes[jax.random.permutation(jax.random.fold_in(rng, 2), count)]


def scatter_about(key, dims, scale, limit, split=(), kind=jnp.bfloat16):
    array = scale * jax.random.normal(key, dims, jnp.float32)
    if split:
        array = array * level_of(key, dims, split, -0.22, 0.18)
    return jnp.clip(array, -limit, limit).astype(kind)


def setup_inputs(seed: int = 0) -> dict:
    keys = jax.random.split(jax.random.key(seed), 9)
    layer_input_rows = scatter_about(keys[0], (TOKENS, D), 1.0, 6.0, ((0, 32), (1, 4)))
    output_gradient_rows = draw_output_gradient_rows(jax.random.fold_in(keys[8], 71), 0)
    adapter_up_weight = scatter_about(keys[2], (OUTPUT_WIDTH, ADAPTER_RANK), OUTPUT_WIDTH ** -0.5, 0.09375, ((0, 4),))
    input_side_projection = scatter_about(keys[3], (D, K1), D ** -0.5, 0.09375, ((0, 4),))
    rank_side_projection = draw_rank_side_projection(jax.random.fold_in(keys[8], 71), 0)
    lengths = ragged(keys[5], S, S * L * 5 // 8, L, 1).astype(jnp.int32)
    program_output_index = jax.random.permutation(keys[6], S).astype(jnp.int32)
    targets = draw_targets(jax.random.fold_in(keys[8], 71), 0)
    return {"layer_input_rows": layer_input_rows, "output_gradient_rows": output_gradient_rows, "adapter_up_weight": adapter_up_weight, "input_side_projection": input_side_projection, "rank_side_projection": rank_side_projection, "lengths": lengths, "program_output_index": program_output_index, "targets": targets}


epsilon = 1e-06

def reference(layer_input_rows, output_gradient_rows, adapter_up_weight, input_side_projection, rank_side_projection, lengths, program_output_index, targets):
    reduced_sums = jnp.dot(output_gradient_rows, adapter_up_weight, preferred_element_type=jnp.float32)
    out_side = jnp.dot(reduced_sums, rank_side_projection.astype(jnp.float32), precision=lax.Precision.HIGHEST)
    in_side = jnp.dot(layer_input_rows, input_side_projection, preferred_element_type=jnp.float32)
    positions = jnp.arange(L, dtype=jnp.int32)
    live_rows = (positions[None, :] < lengths[:, None]).astype(jnp.float32)
    weighted = out_side.reshape(S, L, K2) * live_rows[:, :, None]
    features = jnp.einsum('sla,slb->sab', weighted, in_side.reshape(S, L, K1), precision=lax.Precision.HIGHEST).reshape(S, K)
    squares = lax.optimization_barrier(jnp.sum(features * features, axis=1))
    unit_rows = (features * lax.rsqrt(squares + epsilon)[:, None]).astype(jnp.bfloat16)
    row_order = jnp.argsort(program_output_index).astype(jnp.int32)
    ordered = jnp.take(unit_rows, row_order, axis=0)
    blocks = targets.reshape(N_WIDE, TGTB, K)

    def score_block(target_block):
        wide_block = target_block.astype(jnp.float32)
        target_squares = lax.optimization_barrier(jnp.sum(wide_block * wide_block, axis=1))
        target_unit = (wide_block * lax.rsqrt(target_squares + epsilon)[:, None]).astype(jnp.bfloat16)
        summed = jnp.zeros((S, TGTB), jnp.float32)
        for quarter_index in range(N_NARROW):
            lower = quarter_index * KPART
            quarter_part = jnp.dot(ordered[:, lower:lower + KPART], target_unit[:, lower:lower + KPART].T, preferred_element_type=jnp.float32).astype(jnp.bfloat16)
            summed = summed + quarter_part.astype(jnp.float32)
        return summed * math.sqrt(K)
    stacked = lax.map(score_block, blocks)
    return jnp.transpose(stacked, (1, 0, 2)).reshape(S, TGT)
```

```python
import math

import jax
import jax.numpy as jnp
from jax import lax
from jax.sharding import PartitionSpec as P

epsilon = 1e-06
SCORE_CHUNKS = 4


def program_features(out_side, in_side, lengths, length):
    programs = lengths.shape[0]
    positions = lax.broadcasted_iota(jnp.int32, (programs, length), 1)
    live_rows = (positions < lengths[:, None]).astype(jnp.float32)
    weighted = out_side.reshape(programs, length, -1) * live_rows[:, :, None]
    inputs = in_side.reshape(programs, length, -1)
    outer_sum = jnp.einsum("sla,slb->sab", weighted, inputs, precision=lax.Precision.HIGHEST)
    return outer_sum.reshape(programs, -1)


def normalize_rows(features, squares):
    return (features * lax.rsqrt(squares + epsilon)[:, None]).astype(jnp.bfloat16)


def narrow_sum(own, send_for, count, index, link_type=jnp.bfloat16):
    total = own
    for shift in range(1, count):
        perm = [(i, (i + shift) % count) for i in range(count)]
        piece = send_for((index + shift) % count).astype(link_type)
        total = total + lax.ppermute(piece, "narrow", perm).astype(jnp.float32)
    return total


def shards(
    layer_input_rows,
    output_gradient_rows,
    adapter_up_weight,
    input_side_projection,
    rank_side_projection,
    lengths,
    program_output_index,
    targets,
):
    narrow_count = lax.axis_size("narrow")
    narrow_index = lax.axis_index("narrow")
    programs = lengths.shape[0]
    length = layer_input_rows.shape[0] // programs

    target_wide = targets.astype(jnp.float32)
    target_squares = lax.psum(jnp.sum(target_wide * target_wide, axis=1), "narrow")

    reduced_sums = jnp.dot(
        output_gradient_rows, adapter_up_weight, preferred_element_type=jnp.float32
    )
    out_part = jnp.dot(
        reduced_sums, rank_side_projection.astype(jnp.float32), precision=lax.Precision.HIGHEST
    )
    in_part = jnp.dot(layer_input_rows, input_side_projection, preferred_element_type=jnp.float32)
    quarter_cols = out_part.shape[1] // narrow_count

    def send_for(dest):
        quarter = lax.dynamic_slice_in_dim(out_part, dest * quarter_cols, quarter_cols, 1)
        return jnp.concatenate([quarter, in_part], axis=1)

    summed_parts = narrow_sum(send_for(narrow_index), send_for, narrow_count, narrow_index)
    quarter = summed_parts[:, :quarter_cols]
    in_all = summed_parts[:, quarter_cols:]
    features = program_features(quarter, in_all, lengths, length)
    squares = jnp.sum(features * features, axis=1)
    squares = narrow_sum(squares, lambda dest: squares, narrow_count, narrow_index, jnp.float32)
    unit_rows = normalize_rows(features, squares)
    target_unit = normalize_rows(target_wide, target_squares)
    row_order = jnp.argsort(program_output_index)
    contract = (((1,), (1,)), ((), ()))
    root_count = math.sqrt(float(targets.shape[1] * narrow_count))
    gathered = lax.all_gather(unit_rows, "wide", axis=0, tiled=True)
    permuted = jnp.take(gathered, row_order, axis=0)
    chunk = target_unit.shape[0] // SCORE_CHUNKS
    pieces = []
    for c in range(SCORE_CHUNKS):
        part = lax.dot_general(
            permuted, target_unit[c * chunk:(c + 1) * chunk], contract,
            preferred_element_type=jnp.float32,
        ).astype(jnp.bfloat16)
        pieces.append(
            lax.psum_scatter(part, "narrow", scatter_dimension=0, tiled=True).astype(jnp.float32)
        )
    return jnp.concatenate(pieces, axis=1) * root_count


def solution(mesh):
    return jax.shard_map(
        shards,
        mesh=mesh,
        in_specs=(
            P("wide", "narrow"),
            P("wide", "narrow"),
            P("narrow", None),
            P("narrow", None),
            P(),
            P("wide"),
            P(),
            P("wide", "narrow"),
        ),
        out_specs=P("narrow", "wide"),
        check_vma=False,
    )
```

```python
import functools
import math

import jax
import jax.numpy as jnp
from jax import lax
from jax.experimental import pallas as pl
from jax.experimental.pallas import tpu as pltpu
from jax.sharding import PartitionSpec as P

MESH = pl.DeviceIdType.MESH

epsilon = 1e-06
TILE = 256


def program_features(out_side, in_side, lengths, length):
    programs = lengths.shape[0]
    positions = lax.broadcasted_iota(jnp.int32, (programs, length), 1)
    live_rows = (positions < lengths[:, None]).astype(jnp.float32)
    weighted = out_side.reshape(programs, length, -1) * live_rows[:, :, None]
    inputs = in_side.reshape(programs, length, -1)
    outer_sum = jnp.einsum("sla,slb->sab", weighted, inputs, precision=lax.Precision.HIGHEST)
    return outer_sum.reshape(programs, -1)


def normalize_rows(features, squares):
    return (features * lax.rsqrt(squares + epsilon)[:, None]).astype(jnp.bfloat16)


def narrow_sum(own, send_for, count, index, link_type=jnp.bfloat16):
    total = own
    for shift in range(1, count):
        perm = [(i, (i + shift) % count) for i in range(count)]
        piece = send_for((index + shift) % count).astype(link_type)
        total = total + lax.ppermute(piece, "narrow", perm).astype(jnp.float32)
    return total


def ring_kernel(count, root, u_ref, t_ref, out_ref, send_buf, recv_buf, acc, send_sem, recv_sem):
    me = lax.axis_index("narrow")
    wide = lax.axis_index("wide")
    right, left = lax.rem(me + 1, count), lax.rem(me + count - 1, count)
    rows = out_ref.shape[0]
    half = t_ref.shape[0] // 2
    tiles = rows // TILE

    barrier = pltpu.get_barrier_semaphore()
    for neighbour in (left, right):
        pl.semaphore_signal(barrier, inc=1, device_id=(wide, neighbour), device_id_type=MESH)
    pl.semaphore_wait(barrier, 2)

    def partial_block(block, direction):
        targets = t_ref[direction * half:(direction + 1) * half, :]

        def body(i, carry):
            start = pl.multiple_of(block * rows + i * TILE, TILE)
            lhs = u_ref[pl.ds(start, TILE), :]
            acc[direction, pl.ds(pl.multiple_of(i * TILE, TILE), TILE), :] = lax.dot_general(
                lhs, targets, (((1,), (1,)), ((), ())), preferred_element_type=jnp.float32
            )
            return carry

        lax.fori_loop(0, tiles, body, 0)

    def copy_of(direction, step):
        return pltpu.make_async_remote_copy(
            src_ref=send_buf.at[direction, step],
            dst_ref=recv_buf.at[direction, step],
            send_sem=send_sem.at[direction, step],
            recv_sem=recv_sem.at[direction, step],
            device_id=(wide, right if direction == 0 else left),
            device_id_type=MESH,
        )

    for step in range(count - 1):
        blocks = (lax.rem(me + 2 * count - 1 - step, count), lax.rem(me + 1 + step, count))
        for direction in range(2):
            partial_block(blocks[direction], direction)
        for direction in range(2):
            if step == 0:
                send_buf[direction, step] = acc[direction].astype(jnp.bfloat16)
            else:
                copy_of(direction, step - 1).wait_recv()
                send_buf[direction, step] = (
                    acc[direction] + recv_buf[direction, step - 1].astype(jnp.float32)
                ).astype(jnp.bfloat16)
            copy_of(direction, step).start()
    for direction in range(2):
        partial_block(me, direction)
    for direction in range(2):
        copy_of(direction, count - 2).wait_recv()
        out_ref[:, direction * half:(direction + 1) * half] = (
            acc[direction] + recv_buf[direction, count - 2].astype(jnp.float32)
        ) * root
    for step in range(count - 1):
        for direction in range(2):
            copy_of(direction, step).wait_send()


def ring_scores(permuted, target_unit, count, root):
    programs, depth = permuted.shape
    rows = programs // count
    targets = target_unit.shape[0]
    half = targets // 2
    return pl.pallas_call(
        functools.partial(ring_kernel, count, root),
        out_shape=jax.ShapeDtypeStruct((rows, targets), jnp.float32),
        in_specs=[pl.BlockSpec(memory_space=pltpu.VMEM)] * 2,
        out_specs=pl.BlockSpec(memory_space=pltpu.VMEM),
        scratch_shapes=[
            pltpu.VMEM((2, count - 1, rows, half), jnp.bfloat16),
            pltpu.VMEM((2, count - 1, rows, half), jnp.bfloat16),
            pltpu.VMEM((2, rows, half), jnp.float32),
            pltpu.SemaphoreType.DMA((2, count - 1)),
            pltpu.SemaphoreType.DMA((2, count - 1)),
        ],
        compiler_params=pltpu.CompilerParams(
            collective_id=0, has_side_effects=True, vmem_limit_bytes=60 * 1024 * 1024
        ),
        cost_estimate=pl.CostEstimate(
            flops=2 * programs * depth * targets,
            bytes_accessed=2 * (programs + targets) * depth + 4 * rows * targets,
            transcendentals=0,
        ),
    )(permuted, target_unit)


def shards(
    layer_input_rows,
    output_gradient_rows,
    adapter_up_weight,
    input_side_projection,
    rank_side_projection,
    lengths,
    program_output_index,
    targets,
):
    narrow_count = lax.axis_size("narrow")
    narrow_index = lax.axis_index("narrow")
    programs = lengths.shape[0]
    length = layer_input_rows.shape[0] // programs

    target_wide = targets.astype(jnp.float32)
    target_squares = lax.psum(jnp.sum(target_wide * target_wide, axis=1), "narrow")

    reduced_sums = jnp.dot(
        output_gradient_rows, adapter_up_weight, preferred_element_type=jnp.float32
    )
    out_part = jnp.dot(
        reduced_sums, rank_side_projection.astype(jnp.float32), precision=lax.Precision.HIGHEST
    )
    in_part = jnp.dot(layer_input_rows, input_side_projection, preferred_element_type=jnp.float32)
    quarter_cols = out_part.shape[1] // narrow_count

    def send_for(dest):
        quarter = lax.dynamic_slice_in_dim(out_part, dest * quarter_cols, quarter_cols, 1)
        return jnp.concatenate([quarter, in_part], axis=1)

    summed_parts = narrow_sum(send_for(narrow_index), send_for, narrow_count, narrow_index)
    quarter = summed_parts[:, :quarter_cols]
    in_all = summed_parts[:, quarter_cols:]
    features = program_features(quarter, in_all, lengths, length)
    squares = jnp.sum(features * features, axis=1)
    squares = narrow_sum(squares, lambda dest: squares, narrow_count, narrow_index, jnp.float32)
    unit_rows = normalize_rows(features, squares)
    target_unit = normalize_rows(target_wide, target_squares)
    row_order = jnp.argsort(program_output_index)
    root_count = math.sqrt(float(targets.shape[1] * narrow_count))
    gathered = lax.all_gather(unit_rows, "wide", axis=0, tiled=True)
    permuted = jnp.take(gathered, row_order, axis=0)
    return ring_scores(permuted, target_unit, narrow_count, root_count)


def solution(mesh):
    return jax.shard_map(
        shards,
        mesh=mesh,
        in_specs=(
            P("wide", "narrow"),
            P("wide", "narrow"),
            P("narrow", None),
            P("narrow", None),
            P(),
            P("wide"),
            P(),
            P("wide", "narrow"),
        ),
        out_specs=P("narrow", "wide"),
        check_vma=False,
    )
```

```python
import functools
import math

import jax
import jax.numpy as jnp
from jax import lax
from jax.experimental import pallas as pl
from jax.experimental.pallas import tpu as pltpu
from jax.sharding import PartitionSpec as P

MESH = pl.DeviceIdType.MESH

epsilon = 1e-06
TILE = 256


def program_features(out_side, in_side, lengths, length):
    programs = lengths.shape[0]
    positions = lax.broadcasted_iota(jnp.int32, (programs, length), 1)
    live_rows = (positions < lengths[:, None]).astype(jnp.float32)
    weighted = out_side.reshape(programs, length, -1) * live_rows[:, :, None]
    inputs = in_side.reshape(programs, length, -1)
    outer_sum = jnp.einsum("sla,slb->sab", weighted, inputs, precision=lax.Precision.HIGHEST)
    return outer_sum.reshape(programs, -1)


def normalize_rows(features, squares):
    return (features * lax.rsqrt(squares + epsilon)[:, None]).astype(jnp.bfloat16)


def narrow_sum(own, send_for, count, index, link_type=jnp.bfloat16):
    total = own
    for shift in range(1, count):
        perm = [(i, (i + shift) % count) for i in range(count)]
        piece = send_for((index + shift) % count).astype(link_type)
        total = total + lax.ppermute(piece, "narrow", perm).astype(jnp.float32)
    return total


def ring_kernel(count, root, u_ref, t_ref, out_ref, send_buf, recv_buf, acc, send_sem, recv_sem):
    me = lax.axis_index("narrow")
    wide = lax.axis_index("wide")
    right, left = lax.rem(me + 1, count), lax.rem(me + count - 1, count)
    rows = out_ref.shape[0]
    half = t_ref.shape[0] // 2
    tiles = rows // TILE

    barrier = pltpu.get_barrier_semaphore()
    for neighbour in (left, right):
        pl.semaphore_signal(barrier, inc=1, device_id=(wide, neighbour), device_id_type=MESH)
    pl.semaphore_wait(barrier, 2)

    def partial_block(block, direction):
        targets = t_ref[direction * half:(direction + 1) * half, :]

        def body(i, carry):
            start = pl.multiple_of(block * rows + i * TILE, TILE)
            lhs = u_ref[pl.ds(start, TILE), :]
            acc[direction, pl.ds(pl.multiple_of(i * TILE, TILE), TILE), :] = lax.dot_general(
                lhs, targets, (((1,), (1,)), ((), ())), preferred_element_type=jnp.float32
            )
            return carry

        lax.fori_loop(0, tiles, body, 0)

    def copy_of(direction, step):
        return pltpu.make_async_remote_copy(
            src_ref=send_buf.at[direction, step],
            dst_ref=recv_buf.at[direction, step],
            send_sem=send_sem.at[direction, step],
            recv_sem=recv_sem.at[direction, step],
            device_id=(wide, right if direction == 0 else left),
            device_id_type=MESH,
        )

    for step in range(count - 1):
        blocks = (lax.rem(me + 2 * count - 1 - step, count), lax.rem(me + 1 + step, count))
        for direction in range(2):
            partial_block(blocks[direction], direction)
        for direction in range(2):
            if step == 0:
                send_buf[direction, step] = acc[direction].astype(jnp.bfloat16)
            else:
                copy_of(direction, step - 1).wait_recv()
                send_buf[direction, step] = (
                    acc[direction] + recv_buf[direction, step - 1].astype(jnp.float32)
                ).astype(jnp.bfloat16)
            copy_of(direction, step).start()
    for direction in range(2):
        partial_block(me, direction)
    for direction in range(2):
        copy_of(direction, count - 2).wait_recv()
        out_ref[:, direction * half:(direction + 1) * half] = (
            acc[direction] + recv_buf[direction, count - 2].astype(jnp.float32)
        ) * root
    for step in range(count - 1):
        for direction in range(2):
            copy_of(direction, step).wait_send()


def ring_scores(permuted, target_unit, count, root):
    programs, depth = permuted.shape
    rows = programs // count
    targets = target_unit.shape[0]
    half = targets // 2
    return pl.pallas_call(
        functools.partial(ring_kernel, count, root),
        out_shape=jax.ShapeDtypeStruct((rows, targets), jnp.float32),
        in_specs=[pl.BlockSpec(memory_space=pltpu.VMEM)] * 2,
        out_specs=pl.BlockSpec(memory_space=pltpu.VMEM),
        scratch_shapes=[
            pltpu.VMEM((2, count - 1, rows, half), jnp.bfloat16),
            pltpu.VMEM((2, count - 1, rows, half), jnp.bfloat16),
            pltpu.VMEM((2, rows, half), jnp.float32),
            pltpu.SemaphoreType.DMA((2, count - 1)),
            pltpu.SemaphoreType.DMA((2, count - 1)),
        ],
        compiler_params=pltpu.CompilerParams(
            collective_id=0, has_side_effects=True, vmem_limit_bytes=60 * 1024 * 1024
        ),
        cost_estimate=pl.CostEstimate(
            flops=2 * programs * depth * targets,
            bytes_accessed=2 * (programs + targets) * depth + 4 * rows * targets,
            transcendentals=0,
        ),
    )(permuted, target_unit)


def shards(
    layer_input_rows,
    output_gradient_rows,
    adapter_up_weight,
    input_side_projection,
    rank_side_projection,
    lengths,
    program_output_index,
    targets,
):
    narrow_count = lax.axis_size("narrow")
    narrow_index = lax.axis_index("narrow")
    programs = lengths.shape[0]
    length = layer_input_rows.shape[0] // programs

    target_wide = targets.astype(jnp.float32)
    target_squares = lax.psum(jnp.sum(target_wide * target_wide, axis=1), "narrow")

    reduced_sums = jnp.dot(
        output_gradient_rows, adapter_up_weight, preferred_element_type=jnp.float32
    )
    out_part = jnp.dot(
        reduced_sums, rank_side_projection.astype(jnp.float32), precision=lax.Precision.HIGHEST
    )
    in_part = jnp.dot(layer_input_rows, input_side_projection, preferred_element_type=jnp.float32)
    quarter_cols = out_part.shape[1] // narrow_count

    def send_for(dest):
        quarter = lax.dynamic_slice_in_dim(out_part, dest * quarter_cols, quarter_cols, 1)
        return jnp.concatenate([quarter, in_part], axis=1)

    summed_parts = narrow_sum(send_for(narrow_index), send_for, narrow_count, narrow_index)
    quarter = summed_parts[:, :quarter_cols]
    in_all = summed_parts[:, quarter_cols:]
    features = program_features(quarter, in_all, lengths, length)
    squares = jnp.sum(features * features, axis=1)
    squares = narrow_sum(squares, lambda dest: squares, narrow_count, narrow_index, jnp.float32)
    unit_rows = normalize_rows(features, squares)
    target_unit = normalize_rows(target_wide, target_squares)
    row_order = jnp.argsort(program_output_index)
    root_count = math.sqrt(float(targets.shape[1] * narrow_count))
    gathered = lax.all_gather(unit_rows, "wide", axis=0, tiled=True)
    permuted = gathered.at[row_order].get(mode="promise_in_bounds", unique_indices=True)
    return ring_scores(permuted, target_unit, narrow_count, root_count)


def solution(mesh):
    return jax.shard_map(
        shards,
        mesh=mesh,
        in_specs=(
            P("wide", "narrow"),
            P("wide", "narrow"),
            P("narrow", None),
            P("narrow", None),
            P(),
            P("wide"),
            P(),
            P("wide", "narrow"),
        ),
        out_specs=P("narrow", "wide"),
        check_vma=False,
    )
```

```python
import functools
import math

import jax
import jax.numpy as jnp
from jax import lax
from jax.experimental import pallas as pl
from jax.experimental.pallas import tpu as pltpu
from jax.sharding import PartitionSpec as P

MESH = pl.DeviceIdType.MESH

epsilon = 1e-06
TILE = 256


def program_features(out_side, in_side, lengths, length):
    programs = lengths.shape[0]
    positions = lax.broadcasted_iota(jnp.int32, (programs, length), 1)
    live_rows = (positions < lengths[:, None]).astype(jnp.float32)
    weighted = out_side.reshape(programs, length, -1) * live_rows[:, :, None]
    inputs = in_side.reshape(programs, length, -1)
    outer_sum = jnp.einsum("sla,slb->sab", weighted, inputs, precision=lax.Precision.HIGHEST)
    return outer_sum.reshape(programs, -1)


def normalize_rows(features, squares):
    return (features * lax.rsqrt(squares + epsilon)[:, None]).astype(jnp.bfloat16)


def narrow_sum(own, send_for, count, index, link_type=jnp.bfloat16):
    total = own
    for shift in range(1, count):
        perm = [(i, (i + shift) % count) for i in range(count)]
        piece = send_for((index + shift) % count).astype(link_type)
        total = total + lax.ppermute(piece, "narrow", perm).astype(jnp.float32)
    return total


def ring_kernel(count, root, u_ref, t_ref, out_ref, send_buf, recv_buf, acc, send_sem, recv_sem):
    me = lax.axis_index("narrow")
    right, left = lax.rem(me + 1, count), lax.rem(me + count - 1, count)
    rows = out_ref.shape[0]
    half = t_ref.shape[0] // 2
    tiles = rows // TILE

    barrier = pltpu.get_barrier_semaphore()
    for neighbour in (left, right):
        pl.semaphore_signal(barrier, inc=1, device_id={"narrow": neighbour}, device_id_type=MESH)
    pl.semaphore_wait(barrier, 2)

    def partial_block(block, direction):
        targets = t_ref[direction * half:(direction + 1) * half, :]

        def body(i, carry):
            start = pl.multiple_of(block * rows + i * TILE, TILE)
            lhs = u_ref[pl.ds(start, TILE), :]
            acc[direction, pl.ds(pl.multiple_of(i * TILE, TILE), TILE), :] = lax.dot_general(
                lhs, targets, (((1,), (1,)), ((), ())), preferred_element_type=jnp.float32
            )
            return carry

        lax.fori_loop(0, tiles, body, 0)

    def copy_of(direction, step):
        return pltpu.make_async_remote_copy(
            src_ref=send_buf.at[direction, step],
            dst_ref=recv_buf.at[direction, step],
            send_sem=send_sem.at[direction, step],
            recv_sem=recv_sem.at[direction, step],
            device_id={"narrow": right if direction == 0 else left},
            device_id_type=MESH,
        )

    for step in range(count - 1):
        blocks = (lax.rem(me + 2 * count - 1 - step, count), lax.rem(me + 1 + step, count))
        for direction in range(2):
            partial_block(blocks[direction], direction)
        for direction in range(2):
            if step == 0:
                send_buf[direction, step] = acc[direction].astype(jnp.bfloat16)
            else:
                copy_of(direction, step - 1).wait_recv()
                send_buf[direction, step] = (
                    acc[direction] + recv_buf[direction, step - 1].astype(jnp.float32)
                ).astype(jnp.bfloat16)
            copy_of(direction, step).start()
    for direction in range(2):
        partial_block(me, direction)
    for direction in range(2):
        copy_of(direction, count - 2).wait_recv()
        out_ref[:, direction * half:(direction + 1) * half] = (
            acc[direction] + recv_buf[direction, count - 2].astype(jnp.float32)
        ) * root
    for step in range(count - 1):
        for direction in range(2):
            copy_of(direction, step).wait_send()


def ring_scores(permuted, target_unit, count, root):
    programs, depth = permuted.shape
    rows = programs // count
    targets = target_unit.shape[0]
    half = targets // 2
    return pl.pallas_call(
        functools.partial(ring_kernel, count, root),
        out_shape=jax.ShapeDtypeStruct((rows, targets), jnp.float32),
        in_specs=[pl.BlockSpec(memory_space=pltpu.VMEM)] * 2,
        out_specs=pl.BlockSpec(memory_space=pltpu.VMEM),
        scratch_shapes=[
            pltpu.VMEM((2, count - 1, rows, half), jnp.bfloat16),
            pltpu.VMEM((2, count - 1, rows, half), jnp.bfloat16),
            pltpu.VMEM((2, rows, half), jnp.float32),
            pltpu.SemaphoreType.DMA((2, count - 1)),
            pltpu.SemaphoreType.DMA((2, count - 1)),
        ],
        compiler_params=pltpu.CompilerParams(
            collective_id=0, has_side_effects=True, vmem_limit_bytes=60 * 1024 * 1024
        ),
        cost_estimate=pl.CostEstimate(
            flops=2 * programs * depth * targets,
            bytes_accessed=2 * (programs + targets) * depth + 4 * rows * targets,
            transcendentals=0,
        ),
    )(permuted, target_unit)


def shards(
    layer_input_rows,
    output_gradient_rows,
    adapter_up_weight,
    input_side_projection,
    rank_side_projection,
    lengths,
    program_output_index,
    targets,
):
    narrow_count = lax.axis_size("narrow")
    narrow_index = lax.axis_index("narrow")
    programs = lengths.shape[0]
    length = layer_input_rows.shape[0] // programs

    target_wide = targets.astype(jnp.float32)
    target_squares = lax.psum(jnp.sum(target_wide * target_wide, axis=1), "narrow")

    reduced_sums = jnp.dot(
        output_gradient_rows, adapter_up_weight, preferred_element_type=jnp.float32
    )
    out_part = jnp.dot(
        reduced_sums, rank_side_projection.astype(jnp.float32), precision=lax.Precision.HIGHEST
    )
    in_part = jnp.dot(layer_input_rows, input_side_projection, preferred_element_type=jnp.float32)
    quarter_cols = out_part.shape[1] // narrow_count

    def send_for(dest):
        quarter = lax.dynamic_slice_in_dim(out_part, dest * quarter_cols, quarter_cols, 1)
        return jnp.concatenate([quarter, in_part], axis=1)

    summed_parts = narrow_sum(send_for(narrow_index), send_for, narrow_count, narrow_index)
    quarter = summed_parts[:, :quarter_cols]
    in_all = summed_parts[:, quarter_cols:]
    features = program_features(quarter, in_all, lengths, length)
    squares = jnp.sum(features * features, axis=1)
    squares = narrow_sum(squares, lambda dest: squares, narrow_count, narrow_index, jnp.float32)
    unit_rows = normalize_rows(features, squares)
    target_unit = normalize_rows(target_wide, target_squares)
    row_order = jnp.argsort(program_output_index)
    root_count = math.sqrt(float(targets.shape[1] * narrow_count))
    local = unit_rows.shape[0]
    chips = lax.axis_size("chips")
    cores = lax.axis_size("core")
    gathered = lax.all_gather(unit_rows, "chips", axis=0, tiled=True)
    gathered = lax.all_gather(gathered, "core", axis=0, tiled=True)
    owner = row_order // local
    place = (owner % cores) * (chips * local) + (owner // cores) * local + row_order % local
    permuted = gathered.at[place].get(mode="promise_in_bounds", unique_indices=True)
    return ring_scores(permuted, target_unit, narrow_count, root_count)


def solution(mesh):
    cores = 2
    wide, narrow = mesh.shape["wide"], mesh.shape["narrow"]
    split = jax.sharding.Mesh(
        mesh.devices.reshape(wide // cores, cores, narrow), ("chips", "core", "narrow")
    )
    rows = ("chips", "core")
    return jax.shard_map(
        shards,
        mesh=split,
        in_specs=(
            P(rows, "narrow"),
            P(rows, "narrow"),
            P("narrow", None),
            P("narrow", None),
            P(),
            P(rows),
            P(),
            P(rows, "narrow"),
        ),
        out_specs=P("narrow", rows),
        check_vma=False,
    )
```

```python
import functools
import math

import jax
import jax.numpy as jnp
from jax import lax
from jax.experimental import pallas as pl
from jax.experimental.pallas import tpu as pltpu
from jax.sharding import PartitionSpec as P

MESH = pl.DeviceIdType.MESH

epsilon = 1e-06
TILE = 256


def program_features(out_side, in_side, lengths, length):
    programs = lengths.shape[0]
    positions = lax.broadcasted_iota(jnp.int32, (programs, length), 1)
    live_rows = (positions < lengths[:, None]).astype(jnp.float32)
    weighted = out_side.reshape(programs, length, -1) * live_rows[:, :, None]
    inputs = in_side.reshape(programs, length, -1)
    outer_sum = jnp.einsum("sla,slb->sab", weighted, inputs, precision=lax.Precision.HIGHEST)
    return outer_sum.reshape(programs, -1)


def normalize_rows(features, squares):
    return (features * lax.rsqrt(squares + epsilon)[:, None]).astype(jnp.bfloat16)


def narrow_sum(own, send_for, count, index, link_type=jnp.bfloat16):
    total = own
    for shift in range(1, count):
        perm = [(i, (i + shift) % count) for i in range(count)]
        piece = send_for((index + shift) % count).astype(link_type)
        total = total + lax.ppermute(piece, "narrow", perm).astype(jnp.float32)
    return total


def ring_kernel(count, root, u_ref, t_ref, out_ref, send_buf, recv_buf, acc, send_sem, recv_sem):
    me = lax.axis_index("narrow")
    wide = lax.axis_index("wide")
    right, left = lax.rem(me + 1, count), lax.rem(me + count - 1, count)
    rows = out_ref.shape[0]
    half = t_ref.shape[0] // 2
    tiles = rows // TILE

    barrier = pltpu.get_barrier_semaphore()
    for neighbour in (left, right):
        pl.semaphore_signal(barrier, inc=1, device_id=(wide, neighbour), device_id_type=MESH)
    pl.semaphore_wait(barrier, 2)

    def partial_block(block, direction):
        targets = t_ref[direction * half:(direction + 1) * half, :]

        def body(i, carry):
            start = pl.multiple_of(block * rows + i * TILE, TILE)
            lhs = u_ref[pl.ds(start, TILE), :]
            acc[direction, pl.ds(pl.multiple_of(i * TILE, TILE), TILE), :] = lax.dot_general(
                lhs, targets, (((1,), (1,)), ((), ())), preferred_element_type=jnp.float32
            )
            return carry

        lax.fori_loop(0, tiles, body, 0)

    def copy_of(direction, step):
        return pltpu.make_async_remote_copy(
            src_ref=send_buf.at[direction, step],
            dst_ref=recv_buf.at[direction, step],
            send_sem=send_sem.at[direction, step],
            recv_sem=recv_sem.at[direction, step],
            device_id=(wide, right if direction == 0 else left),
            device_id_type=MESH,
        )

    for step in range(count - 1):
        blocks = (lax.rem(me + 2 * count - 1 - step, count), lax.rem(me + 1 + step, count))
        for direction in range(2):
            partial_block(blocks[direction], direction)
        for direction in range(2):
            if step == 0:
                send_buf[direction, step] = acc[direction].astype(jnp.bfloat16)
            else:
                copy_of(direction, step - 1).wait_recv()
                send_buf[direction, step] = (
                    acc[direction] + recv_buf[direction, step - 1].astype(jnp.float32)
                ).astype(jnp.bfloat16)
            copy_of(direction, step).start()
    for direction in range(2):
        partial_block(me, direction)
    for direction in range(2):
        copy_of(direction, count - 2).wait_recv()
        out_ref[:, direction * half:(direction + 1) * half] = (
            acc[direction] + recv_buf[direction, count - 2].astype(jnp.float32)
        ) * root
    for step in range(count - 1):
        for direction in range(2):
            copy_of(direction, step).wait_send()


def ring_scores(permuted, target_unit, count, root):
    programs, depth = permuted.shape
    rows = programs // count
    targets = target_unit.shape[0]
    half = targets // 2
    return pl.pallas_call(
        functools.partial(ring_kernel, count, root),
        out_shape=jax.ShapeDtypeStruct((rows, targets), jnp.float32),
        in_specs=[pl.BlockSpec(memory_space=pltpu.VMEM)] * 2,
        out_specs=pl.BlockSpec(memory_space=pltpu.VMEM),
        scratch_shapes=[
            pltpu.VMEM((2, count - 1, rows, half), jnp.bfloat16),
            pltpu.VMEM((2, count - 1, rows, half), jnp.bfloat16),
            pltpu.VMEM((2, rows, half), jnp.float32),
            pltpu.SemaphoreType.DMA((2, count - 1)),
            pltpu.SemaphoreType.DMA((2, count - 1)),
        ],
        compiler_params=pltpu.CompilerParams(
            collective_id=0, has_side_effects=True, vmem_limit_bytes=60 * 1024 * 1024
        ),
        cost_estimate=pl.CostEstimate(
            flops=2 * programs * depth * targets,
            bytes_accessed=2 * (programs + targets) * depth + 4 * rows * targets,
            transcendentals=0,
        ),
    )(permuted, target_unit)


RING = 4
SLOT = (0, 2, 3, 1)


def wide_coords(w):
    return w // (2 * RING), (w // 2) % RING, w % 2


def wide_shift(x, axis_of_core, step):
    count = 2 * RING * RING
    perm = []
    for w in range(count):
        y, z, c = wide_coords(w)
        if axis_of_core[c] == "z":
            z = (z + step) % RING
        else:
            y = (y + step) % RING
        perm.append((w, (y * RING + z) * 2 + c))
    return lax.ppermute(x, "wide", perm)


def ring_gather(block, axis_of_core):
    half = block.shape[0] // 2
    from_left = wide_shift(block, axis_of_core, 1)
    from_right = wide_shift(block, axis_of_core, -1)
    far = jnp.concatenate(
        [
            wide_shift(from_left[:half], axis_of_core, 1),
            wide_shift(from_right[half:], axis_of_core, -1),
        ],
        axis=0,
    )
    return jnp.concatenate([block, from_left, from_right, far], axis=0)


def wide_gather(unit_rows, row_order):
    first = ("z", "y")
    second = ("y", "z")
    bundle = ring_gather(unit_rows, first)
    mine = ring_gather(bundle, second)
    partner = lax.ppermute(mine, "wide", [(w, w ^ 1) for w in range(2 * RING * RING)])
    gathered = jnp.concatenate([mine, partner], axis=0)

    local = unit_rows.shape[0]
    y, z, c = wide_coords(lax.axis_index("wide"))
    slot = jnp.asarray(SLOT, jnp.int32)
    owner = row_order // local
    oy, oz, oc = wide_coords(owner)
    dz, dy = (oz - z) % RING, (oy - y) % RING
    first_offset = jnp.where(oc == 0, dz, dy)
    second_offset = jnp.where(oc == 0, dy, dz)
    block = (oc != c) * (RING * RING) + slot[second_offset] * RING + slot[first_offset]
    return gathered, block * local + row_order % local


def shards(
    layer_input_rows,
    output_gradient_rows,
    adapter_up_weight,
    input_side_projection,
    rank_side_projection,
    lengths,
    program_output_index,
    targets,
):
    narrow_count = lax.axis_size("narrow")
    narrow_index = lax.axis_index("narrow")
    programs = lengths.shape[0]
    length = layer_input_rows.shape[0] // programs

    target_wide = targets.astype(jnp.float32)
    target_squares = lax.psum(jnp.sum(target_wide * target_wide, axis=1), "narrow")

    reduced_sums = jnp.dot(
        output_gradient_rows, adapter_up_weight, preferred_element_type=jnp.float32
    )
    out_part = jnp.dot(
        reduced_sums, rank_side_projection.astype(jnp.float32), precision=lax.Precision.HIGHEST
    )
    in_part = jnp.dot(layer_input_rows, input_side_projection, preferred_element_type=jnp.float32)
    quarter_cols = out_part.shape[1] // narrow_count

    def send_for(dest):
        quarter = lax.dynamic_slice_in_dim(out_part, dest * quarter_cols, quarter_cols, 1)
        return jnp.concatenate([quarter, in_part], axis=1)

    summed_parts = narrow_sum(send_for(narrow_index), send_for, narrow_count, narrow_index)
    quarter = summed_parts[:, :quarter_cols]
    in_all = summed_parts[:, quarter_cols:]
    features = program_features(quarter, in_all, lengths, length)
    squares = jnp.sum(features * features, axis=1)
    squares = narrow_sum(squares, lambda dest: squares, narrow_count, narrow_index, jnp.float32)
    unit_rows = normalize_rows(features, squares)
    target_unit = normalize_rows(target_wide, target_squares)
    row_order = jnp.argsort(program_output_index)
    root_count = math.sqrt(float(targets.shape[1] * narrow_count))
    gathered, place = wide_gather(unit_rows, row_order)
    permuted = gathered.at[place].get(mode="promise_in_bounds", unique_indices=True)
    return ring_scores(permuted, target_unit, narrow_count, root_count)


def solution(mesh):
    return jax.shard_map(
        shards,
        mesh=mesh,
        in_specs=(
            P("wide", "narrow"),
            P("wide", "narrow"),
            P("narrow", None),
            P("narrow", None),
            P(),
            P("wide"),
            P(),
            P("wide", "narrow"),
        ),
        out_specs=P("narrow", "wide"),
        check_vma=False,
    )
```

```python
import functools
import math

import jax
import jax.numpy as jnp
from jax import lax
from jax.experimental import pallas as pl
from jax.experimental.pallas import tpu as pltpu
from jax.sharding import PartitionSpec as P

MESH = pl.DeviceIdType.MESH

epsilon = 1e-06
TILE = 256


def program_features(out_side, in_side, lengths, length):
    programs = lengths.shape[0]
    positions = lax.broadcasted_iota(jnp.int32, (programs, length), 1)
    live_rows = (positions < lengths[:, None]).astype(jnp.float32)
    weighted = out_side.reshape(programs, length, -1) * live_rows[:, :, None]
    inputs = in_side.reshape(programs, length, -1)
    outer_sum = jnp.einsum("sla,slb->sab", weighted, inputs, precision=lax.Precision.HIGHEST)
    return outer_sum.reshape(programs, -1)


def normalize_rows(features, squares):
    return (features * lax.rsqrt(squares + epsilon)[:, None]).astype(jnp.bfloat16)


def narrow_sum(own, send_for, count, index, link_type=jnp.bfloat16):
    total = own
    for shift in range(1, count):
        perm = [(i, (i + shift) % count) for i in range(count)]
        piece = send_for((index + shift) % count).astype(link_type)
        total = total + lax.ppermute(piece, "narrow", perm).astype(jnp.float32)
    return total


def ring_kernel(count, root, u_ref, t_ref, out_ref, send_buf, recv_buf, acc, send_sem, recv_sem):
    me = lax.axis_index("narrow")
    wide = lax.axis_index("wide")
    right, left = lax.rem(me + 1, count), lax.rem(me + count - 1, count)
    rows = out_ref.shape[0]
    half = t_ref.shape[0] // 2
    tiles = rows // TILE

    barrier = pltpu.get_barrier_semaphore()
    for neighbour in (left, right):
        pl.semaphore_signal(barrier, inc=1, device_id=(wide, neighbour), device_id_type=MESH)
    pl.semaphore_wait(barrier, 2)

    def partial_block(block, direction):
        targets = t_ref[direction * half:(direction + 1) * half, :]

        def body(i, carry):
            start = pl.multiple_of(block * rows + i * TILE, TILE)
            lhs = u_ref[pl.ds(start, TILE), :]
            acc[direction, pl.ds(pl.multiple_of(i * TILE, TILE), TILE), :] = lax.dot_general(
                lhs, targets, (((1,), (1,)), ((), ())), preferred_element_type=jnp.float32
            )
            return carry

        lax.fori_loop(0, tiles, body, 0)

    def copy_of(direction, step):
        return pltpu.make_async_remote_copy(
            src_ref=send_buf.at[direction, step],
            dst_ref=recv_buf.at[direction, step],
            send_sem=send_sem.at[direction, step],
            recv_sem=recv_sem.at[direction, step],
            device_id=(wide, right if direction == 0 else left),
            device_id_type=MESH,
        )

    for step in range(count - 1):
        blocks = (lax.rem(me + 2 * count - 1 - step, count), lax.rem(me + 1 + step, count))
        for direction in range(2):
            partial_block(blocks[direction], direction)
        for direction in range(2):
            if step == 0:
                send_buf[direction, step] = acc[direction].astype(jnp.bfloat16)
            else:
                copy_of(direction, step - 1).wait_recv()
                send_buf[direction, step] = (
                    acc[direction] + recv_buf[direction, step - 1].astype(jnp.float32)
                ).astype(jnp.bfloat16)
            copy_of(direction, step).start()
    for direction in range(2):
        partial_block(me, direction)
    for direction in range(2):
        copy_of(direction, count - 2).wait_recv()
        out_ref[:, direction * half:(direction + 1) * half] = (
            acc[direction] + recv_buf[direction, count - 2].astype(jnp.float32)
        ) * root
    for step in range(count - 1):
        for direction in range(2):
            copy_of(direction, step).wait_send()


def ring_scores(permuted, target_unit, count, root):
    programs, depth = permuted.shape
    rows = programs // count
    targets = target_unit.shape[0]
    half = targets // 2
    return pl.pallas_call(
        functools.partial(ring_kernel, count, root),
        out_shape=jax.ShapeDtypeStruct((rows, targets), jnp.float32),
        in_specs=[pl.BlockSpec(memory_space=pltpu.VMEM)] * 2,
        out_specs=pl.BlockSpec(memory_space=pltpu.VMEM),
        scratch_shapes=[
            pltpu.VMEM((2, count - 1, rows, half), jnp.bfloat16),
            pltpu.VMEM((2, count - 1, rows, half), jnp.bfloat16),
            pltpu.VMEM((2, rows, half), jnp.float32),
            pltpu.SemaphoreType.DMA((2, count - 1)),
            pltpu.SemaphoreType.DMA((2, count - 1)),
        ],
        compiler_params=pltpu.CompilerParams(
            collective_id=0, has_side_effects=True, vmem_limit_bytes=60 * 1024 * 1024
        ),
        cost_estimate=pl.CostEstimate(
            flops=2 * programs * depth * targets,
            bytes_accessed=2 * (programs + targets) * depth + 4 * rows * targets,
            transcendentals=0,
        ),
    )(permuted, target_unit)


RING = 4
SLOT = (0, 2, 3, 1)


def wide_coords(w):
    return w // (2 * RING), (w // 2) % RING, w % 2


def wide_shift(x, axis_of_core, step):
    count = 2 * RING * RING
    perm = []
    for w in range(count):
        y, z, c = wide_coords(w)
        if axis_of_core[c] == "z":
            z = (z + step) % RING
        else:
            y = (y + step) % RING
        perm.append((w, (y * RING + z) * 2 + c))
    return lax.ppermute(x, "wide", perm)


def ring_gather(block, axis_of_core):
    half = block.shape[0] // 2
    from_left = wide_shift(block, axis_of_core, 1)
    from_right = wide_shift(block, axis_of_core, -1)
    far = jnp.concatenate(
        [
            wide_shift(from_left[:half], axis_of_core, 1),
            wide_shift(from_right[half:], axis_of_core, -1),
        ],
        axis=0,
    )
    return jnp.concatenate([block, from_left, from_right, far], axis=0)


def wide_gather(unit_rows, row_order):
    first = ("z", "y")
    second = ("y", "z")
    bundle = ring_gather(unit_rows, first)
    mine = ring_gather(bundle, second)
    partner = lax.ppermute(mine, "wide", [(w, w ^ 1) for w in range(2 * RING * RING)])
    gathered = jnp.concatenate([mine, partner], axis=0)

    local = unit_rows.shape[0]
    y, z, c = wide_coords(lax.axis_index("wide"))
    slot = jnp.asarray(SLOT, jnp.int32)
    owner = row_order // local
    oy, oz, oc = wide_coords(owner)
    dz, dy = (oz - z) % RING, (oy - y) % RING
    first_offset = jnp.where(oc == 0, dz, dy)
    second_offset = jnp.where(oc == 0, dy, dz)
    block = (oc != c) * (RING * RING) + slot[second_offset] * RING + slot[first_offset]
    return gathered, block * local + row_order % local


def shards(
    layer_input_rows,
    output_gradient_rows,
    adapter_up_weight,
    input_side_projection,
    rank_side_projection,
    lengths,
    program_output_index,
    targets,
):
    narrow_count = lax.axis_size("narrow")
    narrow_index = lax.axis_index("narrow")
    programs = lengths.shape[0]
    length = layer_input_rows.shape[0] // programs

    target_wide = targets.astype(jnp.float32)
    target_squares = jnp.sum(target_wide * target_wide, axis=1)
    target_squares = narrow_sum(
        target_squares, lambda dest: target_squares, narrow_count, narrow_index, jnp.float32
    )
    target_unit = normalize_rows(target_wide, target_squares)
    row_order = jnp.zeros_like(program_output_index).at[program_output_index].set(
        jnp.arange(program_output_index.shape[0], dtype=jnp.int32),
        mode="promise_in_bounds",
        unique_indices=True,
    )

    reduced_sums = jnp.dot(
        output_gradient_rows, adapter_up_weight, preferred_element_type=jnp.float32
    )
    out_part = jnp.dot(
        reduced_sums, rank_side_projection.astype(jnp.float32), precision=lax.Precision.HIGHEST
    )
    in_part = jnp.dot(layer_input_rows, input_side_projection, preferred_element_type=jnp.float32)
    quarter_cols = out_part.shape[1] // narrow_count

    def send_for(dest):
        quarter = lax.dynamic_slice_in_dim(out_part, dest * quarter_cols, quarter_cols, 1)
        return jnp.concatenate([quarter, in_part], axis=1)

    summed_parts = narrow_sum(send_for(narrow_index), send_for, narrow_count, narrow_index)
    summed_parts, target_unit, row_order = lax.optimization_barrier(
        (summed_parts, target_unit, row_order)
    )
    quarter = summed_parts[:, :quarter_cols]
    in_all = summed_parts[:, quarter_cols:]
    features = program_features(quarter, in_all, lengths, length)
    squares = jnp.sum(features * features, axis=1)
    squares = narrow_sum(squares, lambda dest: squares, narrow_count, narrow_index, jnp.float32)
    unit_rows = normalize_rows(features, squares)
    root_count = math.sqrt(float(targets.shape[1] * narrow_count))
    gathered, place = wide_gather(unit_rows, row_order)
    permuted = gathered.at[place].get(mode="promise_in_bounds", unique_indices=True)
    return ring_scores(permuted, target_unit, narrow_count, root_count)


def solution(mesh):
    return jax.shard_map(
        shards,
        mesh=mesh,
        in_specs=(
            P("wide", "narrow"),
            P("wide", "narrow"),
            P("narrow", None),
            P("narrow", None),
            P(),
            P("wide"),
            P(),
            P("wide", "narrow"),
        ),
        out_specs=P("narrow", "wide"),
        check_vma=False,
    )
```

```python
import functools
import math

import jax
import jax.numpy as jnp
from jax import lax
from jax.experimental import pallas as pl
from jax.experimental.pallas import tpu as pltpu
from jax.sharding import PartitionSpec as P

MESH = pl.DeviceIdType.MESH

epsilon = 1e-06
TILE = 256


def program_features(out_side, in_side, lengths, length):
    programs = lengths.shape[0]
    positions = lax.broadcasted_iota(jnp.int32, (programs, length), 1)
    live_rows = (positions < lengths[:, None]).astype(jnp.float32)
    weighted = out_side.reshape(programs, length, -1) * live_rows[:, :, None]
    inputs = in_side.reshape(programs, length, -1)
    outer_sum = jnp.einsum("sla,slb->sab", weighted, inputs, precision=lax.Precision.HIGHEST)
    return outer_sum.reshape(programs, -1)


def normalize_rows(features, squares):
    return (features * lax.rsqrt(squares + epsilon)[:, None]).astype(jnp.bfloat16)


def narrow_sum(own, send_for, count, index, link_type=jnp.bfloat16):
    total = own
    for shift in range(1, count):
        perm = [(i, (i + shift) % count) for i in range(count)]
        piece = send_for((index + shift) % count).astype(link_type)
        total = total + lax.ppermute(piece, "narrow", perm).astype(jnp.float32)
    return total


def ring_kernel(count, root, place_ref, mine_ref, partner_ref, t_ref, out_ref,
                ordered, send_buf, recv_buf, acc, send_sem, recv_sem):
    me = lax.axis_index("narrow")
    right, left = lax.rem(me + 1, count), lax.rem(me + count - 1, count)
    rows = out_ref.shape[0]
    half = t_ref.shape[0] // 2
    held = mine_ref.shape[0]
    tiles = rows // TILE

    barrier = pltpu.get_barrier_semaphore()
    for neighbour in (left, right):
        pl.semaphore_signal(barrier, inc=1, device_id={"narrow": neighbour}, device_id_type=MESH)
    pl.semaphore_wait(barrier, 2)

    def order_block(block):
        def body(i, carry):
            start = pl.multiple_of(block * rows + i * TILE, TILE)
            wanted = place_ref[pl.ds(start, TILE), :]
            columns = lax.broadcasted_iota(jnp.int32, (TILE, held), 1)
            pick_mine = (wanted == columns).astype(jnp.bfloat16)
            pick_partner = (wanted == columns + held).astype(jnp.bfloat16)
            picked = jnp.dot(pick_mine, mine_ref[...], preferred_element_type=jnp.float32)
            picked = picked + jnp.dot(
                pick_partner, partner_ref[...], preferred_element_type=jnp.float32
            )
            ordered[pl.ds(start, TILE), :] = picked.astype(jnp.bfloat16)
            return carry

        lax.fori_loop(0, tiles, body, 0)

    def partial_block(block, direction):
        targets = t_ref[direction * half:(direction + 1) * half, :]

        def body(i, carry):
            start = pl.multiple_of(block * rows + i * TILE, TILE)
            lhs = ordered[pl.ds(start, TILE), :]
            acc[direction, pl.ds(pl.multiple_of(i * TILE, TILE), TILE), :] = lax.dot_general(
                lhs, targets, (((1,), (1,)), ((), ())), preferred_element_type=jnp.float32
            )
            return carry

        lax.fori_loop(0, tiles, body, 0)

    def copy_of(direction, step):
        return pltpu.make_async_remote_copy(
            src_ref=send_buf.at[direction, step],
            dst_ref=recv_buf.at[direction, step],
            send_sem=send_sem.at[direction, step],
            recv_sem=recv_sem.at[direction, step],
            device_id={"narrow": right if direction == 0 else left},
            device_id_type=MESH,
        )

    built = set()

    def need(offset):
        if offset not in built:
            built.add(offset)
            order_block(lax.rem(me + offset, count))

    for step in range(count - 1):
        offsets = ((2 * count - 1 - step) % count, (1 + step) % count)
        for direction in range(2):
            need(offsets[direction])
        for direction in range(2):
            partial_block(lax.rem(me + offsets[direction], count), direction)
        for direction in range(2):
            if step == 0:
                send_buf[direction, step] = acc[direction].astype(jnp.bfloat16)
            else:
                copy_of(direction, step - 1).wait_recv()
                send_buf[direction, step] = (
                    acc[direction] + recv_buf[direction, step - 1].astype(jnp.float32)
                ).astype(jnp.bfloat16)
            copy_of(direction, step).start()
    need(0)
    for direction in range(2):
        partial_block(me, direction)
    for direction in range(2):
        copy_of(direction, count - 2).wait_recv()
        out_ref[:, direction * half:(direction + 1) * half] = (
            acc[direction] + recv_buf[direction, count - 2].astype(jnp.float32)
        ) * root
    for step in range(count - 1):
        for direction in range(2):
            copy_of(direction, step).wait_send()


def ring_scores(place, mine, partner, target_unit, count, root):
    programs = place.shape[0]
    depth = mine.shape[1]
    rows = programs // count
    targets = target_unit.shape[0]
    half = targets // 2
    return pl.pallas_call(
        functools.partial(ring_kernel, count, root),
        out_shape=jax.ShapeDtypeStruct((rows, targets), jnp.float32),
        in_specs=[pl.BlockSpec(memory_space=pltpu.VMEM)] * 4,
        out_specs=pl.BlockSpec(memory_space=pltpu.VMEM),
        scratch_shapes=[
            pltpu.VMEM((programs, depth), jnp.bfloat16),
            pltpu.VMEM((2, count - 1, rows, half), jnp.bfloat16),
            pltpu.VMEM((2, count - 1, rows, half), jnp.bfloat16),
            pltpu.VMEM((2, rows, half), jnp.float32),
            pltpu.SemaphoreType.DMA((2, count - 1)),
            pltpu.SemaphoreType.DMA((2, count - 1)),
        ],
        compiler_params=pltpu.CompilerParams(
            collective_id=0, has_side_effects=True, vmem_limit_bytes=62 * 1024 * 1024
        ),
        cost_estimate=pl.CostEstimate(
            flops=4 * programs * depth * targets,
            bytes_accessed=2 * (2 * programs + targets) * depth + 4 * rows * targets,
            transcendentals=0,
        ),
    )(place.reshape(programs, 1), mine, partner, target_unit)


RING = 4
SLOT = (0, 2, 3, 1)


def wide_coords(w):
    return w // (2 * RING), (w // 2) % RING, w % 2


def wide_shift(x, axis_of_core, step):
    count = 2 * RING * RING
    perm = []
    for w in range(count):
        y, z, c = wide_coords(w)
        if axis_of_core[c] == "z":
            z = (z + step) % RING
        else:
            y = (y + step) % RING
        perm.append((w, (y * RING + z) * 2 + c))
    return lax.ppermute(x, "wide", perm)


def ring_gather(block, axis_of_core):
    half = block.shape[0] // 2
    from_left = wide_shift(block, axis_of_core, 1)
    from_right = wide_shift(block, axis_of_core, -1)
    far = jnp.concatenate(
        [
            wide_shift(from_left[:half], axis_of_core, 1),
            wide_shift(from_right[half:], axis_of_core, -1),
        ],
        axis=0,
    )
    return jnp.concatenate([block, from_left, from_right, far], axis=0)


def wide_gather(unit_rows, row_order):
    first = ("z", "y")
    second = ("y", "z")
    bundle = ring_gather(unit_rows, first)
    mine = ring_gather(bundle, second)
    partner = lax.ppermute(mine, "wide", [(w, w ^ 1) for w in range(2 * RING * RING)])

    local = unit_rows.shape[0]
    y, z, c = wide_coords(lax.axis_index("wide"))
    slot = jnp.asarray(SLOT, jnp.int32)
    owner = row_order // local
    oy, oz, oc = wide_coords(owner)
    dz, dy = (oz - z) % RING, (oy - y) % RING
    first_offset = jnp.where(oc == 0, dz, dy)
    second_offset = jnp.where(oc == 0, dy, dz)
    block = (oc != c) * (RING * RING) + slot[second_offset] * RING + slot[first_offset]
    return mine, partner, block * local + row_order % local


def shards(
    layer_input_rows,
    output_gradient_rows,
    adapter_up_weight,
    input_side_projection,
    rank_side_projection,
    lengths,
    program_output_index,
    targets,
):
    narrow_count = lax.axis_size("narrow")
    narrow_index = lax.axis_index("narrow")
    programs = lengths.shape[0]
    length = layer_input_rows.shape[0] // programs

    target_wide = targets.astype(jnp.float32)
    target_squares = jnp.sum(target_wide * target_wide, axis=1)
    target_squares = narrow_sum(
        target_squares, lambda dest: target_squares, narrow_count, narrow_index, jnp.float32
    )
    target_unit = normalize_rows(target_wide, target_squares)
    row_order = jnp.zeros_like(program_output_index).at[program_output_index].set(
        jnp.arange(program_output_index.shape[0], dtype=jnp.int32),
        mode="promise_in_bounds",
        unique_indices=True,
    )

    reduced_sums = jnp.dot(
        output_gradient_rows, adapter_up_weight, preferred_element_type=jnp.float32
    )
    out_part = jnp.dot(
        reduced_sums, rank_side_projection.astype(jnp.float32), precision=lax.Precision.HIGHEST
    )
    in_part = jnp.dot(layer_input_rows, input_side_projection, preferred_element_type=jnp.float32)
    quarter_cols = out_part.shape[1] // narrow_count

    def send_for(dest):
        quarter = lax.dynamic_slice_in_dim(out_part, dest * quarter_cols, quarter_cols, 1)
        return jnp.concatenate([quarter, in_part], axis=1)

    summed_parts = narrow_sum(send_for(narrow_index), send_for, narrow_count, narrow_index)
    summed_parts, target_unit, row_order = lax.optimization_barrier(
        (summed_parts, target_unit, row_order)
    )
    quarter = summed_parts[:, :quarter_cols]
    in_all = summed_parts[:, quarter_cols:]
    features = program_features(quarter, in_all, lengths, length)
    squares = jnp.sum(features * features, axis=1)
    squares = narrow_sum(squares, lambda dest: squares, narrow_count, narrow_index, jnp.float32)
    unit_rows = normalize_rows(features, squares)
    root_count = math.sqrt(float(targets.shape[1] * narrow_count))
    mine, partner, place = wide_gather(unit_rows, row_order)
    return ring_scores(place, mine, partner, target_unit, narrow_count, root_count)


def solution(mesh):
    return jax.shard_map(
        shards,
        mesh=mesh,
        in_specs=(
            P("wide", "narrow"),
            P("wide", "narrow"),
            P("narrow", None),
            P("narrow", None),
            P(),
            P("wide"),
            P(),
            P("wide", "narrow"),
        ),
        out_specs=P("narrow", "wide"),
        check_vma=False,
    )
```

```python
import functools
import math

import jax
import jax.numpy as jnp
from jax import lax
from jax.experimental import pallas as pl
from jax.experimental.pallas import tpu as pltpu
from jax.sharding import PartitionSpec as P

MESH = pl.DeviceIdType.MESH

epsilon = 1e-06
TILE = 128


def program_features(out_side, in_side, lengths, length):
    programs = lengths.shape[0]
    positions = lax.broadcasted_iota(jnp.int32, (programs, length), 1)
    live_rows = (positions < lengths[:, None]).astype(jnp.float32)
    weighted = out_side.reshape(programs, length, -1) * live_rows[:, :, None]
    inputs = in_side.reshape(programs, length, -1)
    outer_sum = jnp.einsum("sla,slb->sab", weighted, inputs, precision=lax.Precision.HIGHEST)
    return outer_sum.reshape(programs, -1)


def normalize_rows(features, squares):
    return (features * lax.rsqrt(squares + epsilon)[:, None]).astype(jnp.bfloat16)


def narrow_sum(own, send_for, count, index, link_type=jnp.bfloat16):
    total = own
    for shift in range(1, count):
        perm = [(i, (i + shift) % count) for i in range(count)]
        piece = send_for((index + shift) % count).astype(link_type)
        total = total + lax.ppermute(piece, "narrow", perm).astype(jnp.float32)
    return total


def ring_kernel(count, root, place_ref, mine_ref, partner_ref, t_ref, out_ref,
                ordered, send_buf, recv_buf, acc, send_sem, recv_sem):
    me = lax.axis_index("narrow")
    right, left = lax.rem(me + 1, count), lax.rem(me + count - 1, count)
    rows = out_ref.shape[0]
    half = t_ref.shape[0] // 2
    held = mine_ref.shape[0]
    tiles = rows // TILE

    barrier = pltpu.get_barrier_semaphore()
    for neighbour in (left, right):
        pl.semaphore_signal(barrier, inc=1, device_id={"narrow": neighbour}, device_id_type=MESH)
    pl.semaphore_wait(barrier, 2)

    def order_rows(start):
        wanted = place_ref[pl.ds(start, TILE), :]
        columns = lax.broadcasted_iota(jnp.int32, (TILE, held), 1)
        pick_mine = (wanted == columns).astype(jnp.bfloat16)
        pick_partner = (wanted == columns + held).astype(jnp.bfloat16)
        picked = jnp.dot(pick_mine, mine_ref[...], preferred_element_type=jnp.float32)
        picked = picked + jnp.dot(pick_partner, partner_ref[...], preferred_element_type=jnp.float32)
        ordered[pl.ds(start, TILE), :] = picked.astype(jnp.bfloat16)

    def partial_rows(start, direction, part):
        targets = t_ref[direction * half:(direction + 1) * half, :]
        acc[direction, part] = lax.dot_general(
            ordered[pl.ds(start, TILE), :], targets, (((1,), (1,)), ((), ())),
            preferred_element_type=jnp.float32,
        )

    def copy_of(direction, step, part):
        return pltpu.make_async_remote_copy(
            src_ref=send_buf.at[direction, step, part],
            dst_ref=recv_buf.at[direction, step, part],
            send_sem=send_sem.at[direction, step, part],
            recv_sem=recv_sem.at[direction, step, part],
            device_id={"narrow": right if direction == 0 else left},
            device_id_type=MESH,
        )

    built = set()
    for step in range(count - 1):
        offsets = ((2 * count - 1 - step) % count, (1 + step) % count)
        fresh = [offset not in built for offset in offsets]
        built.update(offsets)

        def body(part, carry, step=step, offsets=offsets, fresh=fresh):
            for direction in range(2):
                start = pl.multiple_of(lax.rem(me + offsets[direction], count) * rows + part * TILE, TILE)
                if fresh[direction] and not (direction == 1 and offsets[1] == offsets[0]):
                    order_rows(start)
                partial_rows(start, direction, part)
                if step == 0:
                    send_buf[direction, step, part] = acc[direction, part].astype(jnp.bfloat16)
                else:
                    copy_of(direction, step - 1, part).wait_recv()
                    send_buf[direction, step, part] = (
                        acc[direction, part] + recv_buf[direction, step - 1, part].astype(jnp.float32)
                    ).astype(jnp.bfloat16)
                copy_of(direction, step, part).start()
            return carry

        lax.fori_loop(0, tiles, body, 0)

    def last(part, carry):
        start = pl.multiple_of(me * rows + part * TILE, TILE)
        order_rows(start)
        for direction in range(2):
            partial_rows(start, direction, part)
            copy_of(direction, count - 2, part).wait_recv()
            out_ref[pl.ds(start - me * rows, TILE), direction * half:(direction + 1) * half] = (
                acc[direction, part] + recv_buf[direction, count - 2, part].astype(jnp.float32)
            ) * root
        return carry

    lax.fori_loop(0, tiles, last, 0)

    def drain(part, carry):
        for step in range(count - 1):
            for direction in range(2):
                copy_of(direction, step, part).wait_send()
        return carry

    lax.fori_loop(0, tiles, drain, 0)


def ring_scores(place, mine, partner, target_unit, count, root):
    programs = place.shape[0]
    depth = mine.shape[1]
    rows = programs // count
    targets = target_unit.shape[0]
    half = targets // 2
    return pl.pallas_call(
        functools.partial(ring_kernel, count, root),
        out_shape=jax.ShapeDtypeStruct((rows, targets), jnp.float32),
        in_specs=[pl.BlockSpec(memory_space=pltpu.VMEM)] * 4,
        out_specs=pl.BlockSpec(memory_space=pltpu.VMEM),
        scratch_shapes=[
            pltpu.VMEM((programs, depth), jnp.bfloat16),
            pltpu.VMEM((2, count - 1, rows // TILE, TILE, half), jnp.bfloat16),
            pltpu.VMEM((2, count - 1, rows // TILE, TILE, half), jnp.bfloat16),
            pltpu.VMEM((2, rows // TILE, TILE, half), jnp.float32),
            pltpu.SemaphoreType.DMA((2, count - 1, rows // TILE)),
            pltpu.SemaphoreType.DMA((2, count - 1, rows // TILE)),
        ],
        compiler_params=pltpu.CompilerParams(
            collective_id=0, has_side_effects=True, vmem_limit_bytes=62 * 1024 * 1024
        ),
        cost_estimate=pl.CostEstimate(
            flops=4 * programs * depth * targets,
            bytes_accessed=2 * (2 * programs + targets) * depth + 4 * rows * targets,
            transcendentals=0,
        ),
    )(place.reshape(programs, 1), mine, partner, target_unit)


RING = 4
SLOT = (0, 2, 3, 1)


def wide_coords(w):
    return w // (2 * RING), (w // 2) % RING, w % 2


def wide_shift(x, axis_of_core, step):
    count = 2 * RING * RING
    perm = []
    for w in range(count):
        y, z, c = wide_coords(w)
        if axis_of_core[c] == "z":
            z = (z + step) % RING
        else:
            y = (y + step) % RING
        perm.append((w, (y * RING + z) * 2 + c))
    return lax.ppermute(x, "wide", perm)


def ring_gather(block, axis_of_core):
    half = block.shape[0] // 2
    from_left = wide_shift(block, axis_of_core, 1)
    from_right = wide_shift(block, axis_of_core, -1)
    far = jnp.concatenate(
        [
            wide_shift(from_left[:half], axis_of_core, 1),
            wide_shift(from_right[half:], axis_of_core, -1),
        ],
        axis=0,
    )
    return jnp.concatenate([block, from_left, from_right, far], axis=0)


def wide_gather(unit_rows, row_order):
    first = ("z", "y")
    second = ("y", "z")
    bundle = ring_gather(unit_rows, first)
    mine = ring_gather(bundle, second)
    partner = lax.ppermute(mine, "wide", [(w, w ^ 1) for w in range(2 * RING * RING)])

    local = unit_rows.shape[0]
    y, z, c = wide_coords(lax.axis_index("wide"))
    slot = jnp.asarray(SLOT, jnp.int32)
    owner = row_order // local
    oy, oz, oc = wide_coords(owner)
    dz, dy = (oz - z) % RING, (oy - y) % RING
    first_offset = jnp.where(oc == 0, dz, dy)
    second_offset = jnp.where(oc == 0, dy, dz)
    block = (oc != c) * (RING * RING) + slot[second_offset] * RING + slot[first_offset]
    return mine, partner, block * local + row_order % local


def shards(
    layer_input_rows,
    output_gradient_rows,
    adapter_up_weight,
    input_side_projection,
    rank_side_projection,
    lengths,
    program_output_index,
    targets,
):
    narrow_count = lax.axis_size("narrow")
    narrow_index = lax.axis_index("narrow")
    programs = lengths.shape[0]
    length = layer_input_rows.shape[0] // programs

    target_wide = targets.astype(jnp.float32)
    target_squares = jnp.sum(target_wide * target_wide, axis=1)
    target_squares = narrow_sum(
        target_squares, lambda dest: target_squares, narrow_count, narrow_index, jnp.float32
    )
    target_unit = normalize_rows(target_wide, target_squares)
    row_order = jnp.zeros_like(program_output_index).at[program_output_index].set(
        jnp.arange(program_output_index.shape[0], dtype=jnp.int32),
        mode="promise_in_bounds",
        unique_indices=True,
    )

    reduced_sums = jnp.dot(
        output_gradient_rows, adapter_up_weight, preferred_element_type=jnp.float32
    )
    out_part = jnp.dot(
        reduced_sums, rank_side_projection.astype(jnp.float32), precision=lax.Precision.HIGHEST
    )
    in_part = jnp.dot(layer_input_rows, input_side_projection, preferred_element_type=jnp.float32)
    quarter_cols = out_part.shape[1] // narrow_count

    def send_for(dest):
        quarter = lax.dynamic_slice_in_dim(out_part, dest * quarter_cols, quarter_cols, 1)
        return jnp.concatenate([quarter, in_part], axis=1)

    summed_parts = narrow_sum(send_for(narrow_index), send_for, narrow_count, narrow_index)
    summed_parts, target_unit, row_order = lax.optimization_barrier(
        (summed_parts, target_unit, row_order)
    )
    quarter = summed_parts[:, :quarter_cols]
    in_all = summed_parts[:, quarter_cols:]
    features = program_features(quarter, in_all, lengths, length)
    squares = jnp.sum(features * features, axis=1)
    squares = narrow_sum(squares, lambda dest: squares, narrow_count, narrow_index, jnp.float32)
    unit_rows = normalize_rows(features, squares)
    root_count = math.sqrt(float(targets.shape[1] * narrow_count))
    mine, partner, place = wide_gather(unit_rows, row_order)
    return ring_scores(place, mine, partner, target_unit, narrow_count, root_count)


def solution(mesh):
    return jax.shard_map(
        shards,
        mesh=mesh,
        in_specs=(
            P("wide", "narrow"),
            P("wide", "narrow"),
            P("narrow", None),
            P("narrow", None),
            P(),
            P("wide"),
            P(),
            P("wide", "narrow"),
        ),
        out_specs=P("narrow", "wide"),
        check_vma=False,
    )
```

```python
import functools
import math

import jax
import jax.numpy as jnp
from jax import lax
from jax.experimental import pallas as pl
from jax.experimental.pallas import tpu as pltpu
from jax.sharding import PartitionSpec as P

MESH = pl.DeviceIdType.MESH

epsilon = 1e-06
TILE = 128


def program_features(out_side, in_side, lengths, length):
    programs = lengths.shape[0]
    positions = lax.broadcasted_iota(jnp.int32, (programs, length), 1)
    live_rows = (positions < lengths[:, None]).astype(jnp.float32)
    weighted = out_side.reshape(programs, length, -1) * live_rows[:, :, None]
    inputs = in_side.reshape(programs, length, -1)
    outer_sum = jnp.einsum("sla,slb->sab", weighted, inputs, precision=lax.Precision.HIGHEST)
    return outer_sum.reshape(programs, -1)


def normalize_rows(features, squares):
    return (features * lax.rsqrt(squares + epsilon)[:, None]).astype(jnp.bfloat16)


def narrow_sum(own, send_for, count, index, link_type=jnp.bfloat16):
    total = own
    for shift in range(1, count):
        perm = [(i, (i + shift) % count) for i in range(count)]
        piece = send_for((index + shift) % count).astype(link_type)
        total = total + lax.ppermute(piece, "narrow", perm).astype(jnp.float32)
    return total


def ring_kernel(count, root, place_ref, scale_ref, mine_ref, partner_ref, t_ref, out_ref,
                ordered, send_buf, recv_buf, acc, send_sem, recv_sem):
    me = lax.axis_index("narrow")
    right, left = lax.rem(me + 1, count), lax.rem(me + count - 1, count)
    rows = out_ref.shape[0]
    half = t_ref.shape[0] // 2
    held = mine_ref.shape[0]
    tiles = rows // TILE

    barrier = pltpu.get_barrier_semaphore()
    for neighbour in (left, right):
        pl.semaphore_signal(barrier, inc=1, device_id={"narrow": neighbour}, device_id_type=MESH)
    pl.semaphore_wait(barrier, 2)

    def order_rows(start):
        wanted = place_ref[pl.ds(start, TILE), :]
        columns = lax.broadcasted_iota(jnp.int32, (TILE, held), 1)
        pick_mine = (wanted == columns).astype(jnp.bfloat16)
        pick_partner = (wanted == columns + held).astype(jnp.bfloat16)
        picked = jnp.dot(pick_mine, mine_ref[...], preferred_element_type=jnp.float32)
        picked = picked + jnp.dot(pick_partner, partner_ref[...], preferred_element_type=jnp.float32)
        ordered[pl.ds(start, TILE), :] = (picked * scale_ref[pl.ds(start, TILE), :]).astype(
            jnp.bfloat16
        )

    def partial_rows(start, direction, part):
        targets = t_ref[direction * half:(direction + 1) * half, :]
        acc[direction, part] = lax.dot_general(
            ordered[pl.ds(start, TILE), :], targets, (((1,), (1,)), ((), ())),
            preferred_element_type=jnp.float32,
        )

    def copy_of(direction, step, part):
        return pltpu.make_async_remote_copy(
            src_ref=send_buf.at[direction, step, part],
            dst_ref=recv_buf.at[direction, step, part],
            send_sem=send_sem.at[direction, step, part],
            recv_sem=recv_sem.at[direction, step, part],
            device_id={"narrow": right if direction == 0 else left},
            device_id_type=MESH,
        )

    built = set()
    for step in range(count - 1):
        offsets = ((2 * count - 1 - step) % count, (1 + step) % count)
        fresh = [offset not in built for offset in offsets]
        built.update(offsets)

        def body(part, carry, step=step, offsets=offsets, fresh=fresh):
            for direction in range(2):
                start = pl.multiple_of(lax.rem(me + offsets[direction], count) * rows + part * TILE, TILE)
                if fresh[direction] and not (direction == 1 and offsets[1] == offsets[0]):
                    order_rows(start)
                partial_rows(start, direction, part)
                if step == 0:
                    send_buf[direction, step, part] = acc[direction, part].astype(jnp.bfloat16)
                else:
                    copy_of(direction, step - 1, part).wait_recv()
                    send_buf[direction, step, part] = (
                        acc[direction, part] + recv_buf[direction, step - 1, part].astype(jnp.float32)
                    ).astype(jnp.bfloat16)
                copy_of(direction, step, part).start()
            return carry

        lax.fori_loop(0, tiles, body, 0)

    def last(part, carry):
        start = pl.multiple_of(me * rows + part * TILE, TILE)
        order_rows(start)
        for direction in range(2):
            partial_rows(start, direction, part)
            copy_of(direction, count - 2, part).wait_recv()
            out_ref[pl.ds(start - me * rows, TILE), direction * half:(direction + 1) * half] = (
                acc[direction, part] + recv_buf[direction, count - 2, part].astype(jnp.float32)
            ) * root
        return carry

    lax.fori_loop(0, tiles, last, 0)

    def drain(part, carry):
        for step in range(count - 1):
            for direction in range(2):
                copy_of(direction, step, part).wait_send()
        return carry

    lax.fori_loop(0, tiles, drain, 0)


def ring_scores(place, scale, mine, partner, target_unit, count, root):
    programs = place.shape[0]
    depth = mine.shape[1]
    rows = programs // count
    targets = target_unit.shape[0]
    half = targets // 2
    return pl.pallas_call(
        functools.partial(ring_kernel, count, root),
        out_shape=jax.ShapeDtypeStruct((rows, targets), jnp.float32),
        in_specs=[pl.BlockSpec(memory_space=pltpu.VMEM)] * 5,
        out_specs=pl.BlockSpec(memory_space=pltpu.VMEM),
        scratch_shapes=[
            pltpu.VMEM((programs, depth), jnp.bfloat16),
            pltpu.VMEM((2, count - 1, rows // TILE, TILE, half), jnp.bfloat16),
            pltpu.VMEM((2, count - 1, rows // TILE, TILE, half), jnp.bfloat16),
            pltpu.VMEM((2, rows // TILE, TILE, half), jnp.float32),
            pltpu.SemaphoreType.DMA((2, count - 1, rows // TILE)),
            pltpu.SemaphoreType.DMA((2, count - 1, rows // TILE)),
        ],
        compiler_params=pltpu.CompilerParams(
            collective_id=0, has_side_effects=True, vmem_limit_bytes=62 * 1024 * 1024
        ),
        cost_estimate=pl.CostEstimate(
            flops=4 * programs * depth * targets,
            bytes_accessed=2 * (2 * programs + targets) * depth + 4 * rows * targets,
            transcendentals=0,
        ),
    )(place.reshape(programs, 1), scale.reshape(programs, 1), mine, partner, target_unit)


RING = 4
SLOT = (0, 2, 3, 1)


def wide_coords(w):
    return w // (2 * RING), (w // 2) % RING, w % 2


def wide_shift(x, axis_of_core, step):
    count = 2 * RING * RING
    perm = []
    for w in range(count):
        y, z, c = wide_coords(w)
        if axis_of_core[c] == "z":
            z = (z + step) % RING
        else:
            y = (y + step) % RING
        perm.append((w, (y * RING + z) * 2 + c))
    return lax.ppermute(x, "wide", perm)


def ring_gather(block, axis_of_core):
    half = block.shape[0] // 2
    from_left = wide_shift(block, axis_of_core, 1)
    from_right = wide_shift(block, axis_of_core, -1)
    far = jnp.concatenate(
        [
            wide_shift(from_left[:half], axis_of_core, 1),
            wide_shift(from_right[half:], axis_of_core, -1),
        ],
        axis=0,
    )
    return jnp.concatenate([block, from_left, from_right, far], axis=0)


def wide_gather(unit_rows):
    first = ("z", "y")
    second = ("y", "z")
    bundle = ring_gather(unit_rows, first)
    mine = ring_gather(bundle, second)
    partner = lax.ppermute(mine, "wide", [(w, w ^ 1) for w in range(2 * RING * RING)])
    return mine, partner


def gathered_place(row_order, local):
    y, z, c = wide_coords(lax.axis_index("wide"))
    slot = jnp.asarray(SLOT, jnp.int32)
    owner = row_order // local
    oy, oz, oc = wide_coords(owner)
    dz, dy = (oz - z) % RING, (oy - y) % RING
    first_offset = jnp.where(oc == 0, dz, dy)
    second_offset = jnp.where(oc == 0, dy, dz)
    block = (oc != c) * (RING * RING) + slot[second_offset] * RING + slot[first_offset]
    return block * local + row_order % local


def shards(
    layer_input_rows,
    output_gradient_rows,
    adapter_up_weight,
    input_side_projection,
    rank_side_projection,
    lengths,
    program_output_index,
    targets,
):
    narrow_count = lax.axis_size("narrow")
    narrow_index = lax.axis_index("narrow")
    programs = lengths.shape[0]
    length = layer_input_rows.shape[0] // programs

    target_wide = targets.astype(jnp.float32)
    target_squares = jnp.sum(target_wide * target_wide, axis=1)
    target_squares = narrow_sum(
        target_squares, lambda dest: target_squares, narrow_count, narrow_index, jnp.float32
    )
    target_unit = normalize_rows(target_wide, target_squares)
    row_order = jnp.zeros_like(program_output_index).at[program_output_index].set(
        jnp.arange(program_output_index.shape[0], dtype=jnp.int32),
        mode="promise_in_bounds",
        unique_indices=True,
    )

    reduced_sums = jnp.dot(
        output_gradient_rows, adapter_up_weight, preferred_element_type=jnp.float32
    )
    out_part = jnp.dot(
        reduced_sums, rank_side_projection.astype(jnp.float32), precision=lax.Precision.HIGHEST
    )
    in_part = jnp.dot(layer_input_rows, input_side_projection, preferred_element_type=jnp.float32)
    quarter_cols = out_part.shape[1] // narrow_count

    def send_for(dest):
        quarter = lax.dynamic_slice_in_dim(out_part, dest * quarter_cols, quarter_cols, 1)
        return jnp.concatenate([quarter, in_part], axis=1)

    summed_parts = narrow_sum(send_for(narrow_index), send_for, narrow_count, narrow_index)
    summed_parts, target_unit, row_order = lax.optimization_barrier(
        (summed_parts, target_unit, row_order)
    )
    quarter = summed_parts[:, :quarter_cols]
    in_all = summed_parts[:, quarter_cols:]
    features = program_features(quarter, in_all, lengths, length)
    mine, partner = wide_gather(features.astype(jnp.bfloat16))
    squares = jnp.sum(features * features, axis=1)
    squares = narrow_sum(squares, lambda dest: squares, narrow_count, narrow_index, jnp.float32)
    scale = lax.rsqrt(squares + epsilon)[:, None]
    scale_mine, scale_partner = wide_gather(scale)
    place = gathered_place(row_order, features.shape[0])
    scale = jnp.concatenate([scale_mine, scale_partner], axis=0)[place, 0]
    root_count = math.sqrt(float(targets.shape[1] * narrow_count))
    return ring_scores(place, scale, mine, partner, target_unit, narrow_count, root_count)


def solution(mesh):
    return jax.shard_map(
        shards,
        mesh=mesh,
        in_specs=(
            P("wide", "narrow"),
            P("wide", "narrow"),
            P("narrow", None),
            P("narrow", None),
            P(),
            P("wide"),
            P(),
            P("wide", "narrow"),
        ),
        out_specs=P("narrow", "wide"),
        check_vma=False,
    )
```

```python
import functools
import math

import jax
import jax.numpy as jnp
from jax import lax
from jax.experimental import pallas as pl
from jax.experimental.pallas import tpu as pltpu
from jax.sharding import PartitionSpec as P

MESH = pl.DeviceIdType.MESH

epsilon = 1e-06
TILE = 128


def program_features(out_side, in_side, lengths, length):
    programs = lengths.shape[0]
    positions = lax.broadcasted_iota(jnp.int32, (programs, length), 1)
    live_rows = (positions < lengths[:, None]).astype(jnp.float32)
    weighted = out_side.reshape(programs, length, -1) * live_rows[:, :, None]
    inputs = in_side.reshape(programs, length, -1)
    outer_sum = jnp.einsum("sla,slb->sab", weighted, inputs, precision=lax.Precision.HIGHEST)
    return outer_sum.reshape(programs, -1)


def normalize_rows(features, squares):
    return (features * lax.rsqrt(squares + epsilon)[:, None]).astype(jnp.bfloat16)


def narrow_sum(own, send_for, count, index, link_type=jnp.bfloat16):
    total = own
    for shift in range(1, count):
        perm = [(i, (i + shift) % count) for i in range(count)]
        piece = send_for((index + shift) % count).astype(link_type)
        total = total + lax.ppermute(piece, "narrow", perm).astype(jnp.float32)
    return total


def ring_kernel(count, root, place_ref, rows_ref, t_ref, out_ref, gathered,
                ordered, send_buf, recv_buf, acc, send_sem, recv_sem, wide_send, wide_recv):
    me = lax.axis_index("narrow")
    right, left = lax.rem(me + 1, count), lax.rem(me + count - 1, count)
    rows = out_ref.shape[0]
    half = t_ref.shape[0] // 2
    tiles = rows // TILE
    local = rows_ref.shape[0]
    everyone = gathered.shape[0]

    wide = lax.axis_index("wide")
    y, z, core = wide // (2 * RING), (wide // 2) % RING, wide % 2

    def wide_peer(first_axis, step):
        along_z = (1 - core) if first_axis else core
        along_y = 1 - along_z
        return {"wide": (lax.rem(y + RING + step * along_y, RING) * RING
                         + lax.rem(z + RING + step * along_z, RING)) * 2 + core}

    partner = {"wide": wide + 1 - 2 * core}
    peers = [wide_peer(True, 1), wide_peer(True, -1), wide_peer(False, 1), wide_peer(False, -1), partner]

    barrier = pltpu.get_barrier_semaphore()
    for neighbour in (left, right):
        pl.semaphore_signal(barrier, inc=1, device_id={"narrow": neighbour}, device_id_type=MESH)
    for peer in peers:
        pl.semaphore_signal(barrier, inc=1, device_id=peer, device_id_type=MESH)
    pl.semaphore_wait(barrier, 2 + len(peers))

    def wide_copy(index, src, dst_start, size, peer):
        return pltpu.make_async_remote_copy(
            src_ref=src,
            dst_ref=gathered.at[pl.ds(dst_start, size)],
            send_sem=wide_send.at[index],
            recv_sem=wide_recv.at[index],
            device_id=peer,
            device_id_type=MESH,
        )

    def at(start, size):
        return gathered.at[pl.ds(start, size)]

    block, bundle = local, RING * local
    part_half, bundle_half = local // 2, bundle // 2
    plan = []
    plan.append(wide_copy(0, rows_ref, SLOT[RING - 1] * block, block, peers[0]))
    plan.append(wide_copy(1, rows_ref, SLOT[1] * block, block, peers[1]))
    gathered[0:block, :] = rows_ref[...]
    plan[0].start()
    plan[1].start()
    plan[0].wait_recv()
    plan.append(wide_copy(2, at(SLOT[RING - 1] * block, part_half), SLOT[2] * block, part_half, peers[0]))
    plan[2].start()
    plan[1].wait_recv()
    plan.append(wide_copy(3, at(SLOT[1] * block + part_half, part_half),
                          SLOT[2] * block + part_half, part_half, peers[1]))
    plan[3].start()
    plan[2].wait_recv()
    plan[3].wait_recv()
    plan.append(wide_copy(4, at(0, bundle), SLOT[RING - 1] * bundle, bundle, peers[2]))
    plan.append(wide_copy(5, at(0, bundle), SLOT[1] * bundle, bundle, peers[3]))
    plan.append(wide_copy(6, at(0, bundle), everyone // 2, bundle, partner))
    for copy in plan[4:7]:
        copy.start()
    plan[4].wait_recv()
    plan.append(wide_copy(7, at(SLOT[RING - 1] * bundle, bundle_half), SLOT[2] * bundle, bundle_half, peers[2]))
    plan.append(wide_copy(8, at(SLOT[RING - 1] * bundle, bundle), everyone // 2 + SLOT[RING - 1] * bundle,
                          bundle, partner))
    plan[7].start()
    plan[8].start()
    plan[5].wait_recv()
    plan.append(wide_copy(9, at(SLOT[1] * bundle + bundle_half, bundle_half),
                          SLOT[2] * bundle + bundle_half, bundle_half, peers[3]))
    plan.append(wide_copy(10, at(SLOT[1] * bundle, bundle), everyone // 2 + SLOT[1] * bundle,
                          bundle, partner))
    plan[9].start()
    plan[10].start()
    plan[7].wait_recv()
    plan[9].wait_recv()
    plan.append(wide_copy(11, at(SLOT[2] * bundle, bundle), everyone // 2 + SLOT[2] * bundle,
                          bundle, partner))
    plan[11].start()
    for index in (6, 8, 10, 11):
        plan[index].wait_recv()

    def order_rows(start):
        wanted = place_ref[pl.ds(start, TILE), :]
        columns = lax.broadcasted_iota(jnp.int32, (TILE, everyone), 1)
        pick = (wanted == columns).astype(jnp.bfloat16)
        picked = jnp.dot(pick, gathered[...], preferred_element_type=jnp.float32)
        ordered[pl.ds(start, TILE), :] = picked.astype(jnp.bfloat16)

    def partial_rows(start, direction, part):
        targets = t_ref[direction * half:(direction + 1) * half, :]
        acc[direction, part] = lax.dot_general(
            ordered[pl.ds(start, TILE), :], targets, (((1,), (1,)), ((), ())),
            preferred_element_type=jnp.float32,
        )

    def copy_of(direction, step, part):
        return pltpu.make_async_remote_copy(
            src_ref=send_buf.at[direction, step, part],
            dst_ref=recv_buf.at[direction, step, part],
            send_sem=send_sem.at[direction, step, part],
            recv_sem=recv_sem.at[direction, step, part],
            device_id={"narrow": right if direction == 0 else left},
            device_id_type=MESH,
        )

    built = set()
    for step in range(count - 1):
        offsets = ((2 * count - 1 - step) % count, (1 + step) % count)
        fresh = [offset not in built for offset in offsets]
        built.update(offsets)

        def body(part, carry, step=step, offsets=offsets, fresh=fresh):
            for direction in range(2):
                start = pl.multiple_of(lax.rem(me + offsets[direction], count) * rows + part * TILE, TILE)
                if fresh[direction] and not (direction == 1 and offsets[1] == offsets[0]):
                    order_rows(start)
                partial_rows(start, direction, part)
                if step == 0:
                    send_buf[direction, step, part] = acc[direction, part].astype(jnp.bfloat16)
                else:
                    copy_of(direction, step - 1, part).wait_recv()
                    send_buf[direction, step, part] = (
                        acc[direction, part] + recv_buf[direction, step - 1, part].astype(jnp.float32)
                    ).astype(jnp.bfloat16)
                copy_of(direction, step, part).start()
            return carry

        lax.fori_loop(0, tiles, body, 0)

    def last(part, carry):
        start = pl.multiple_of(me * rows + part * TILE, TILE)
        order_rows(start)
        for direction in range(2):
            partial_rows(start, direction, part)
            copy_of(direction, count - 2, part).wait_recv()
            out_ref[pl.ds(start - me * rows, TILE), direction * half:(direction + 1) * half] = (
                acc[direction, part] + recv_buf[direction, count - 2, part].astype(jnp.float32)
            ) * root
        return carry

    lax.fori_loop(0, tiles, last, 0)

    def drain(part, carry):
        for step in range(count - 1):
            for direction in range(2):
                copy_of(direction, step, part).wait_send()
        return carry

    lax.fori_loop(0, tiles, drain, 0)
    for copy in plan:
        copy.wait_send()


def ring_scores(place, unit_rows, target_unit, count, root):
    programs = place.shape[0]
    depth = unit_rows.shape[1]
    rows = programs // count
    targets = target_unit.shape[0]
    half = targets // 2
    return pl.pallas_call(
        functools.partial(ring_kernel, count, root),
        out_shape=jax.ShapeDtypeStruct((rows, targets), jnp.float32),
        in_specs=[pl.BlockSpec(memory_space=pltpu.VMEM)] * 3,
        out_specs=pl.BlockSpec(memory_space=pltpu.VMEM),
        scratch_shapes=[
            pltpu.VMEM((programs, depth), jnp.bfloat16),
            pltpu.VMEM((programs, depth), jnp.bfloat16),
            pltpu.VMEM((2, count - 1, rows // TILE, TILE, half), jnp.bfloat16),
            pltpu.VMEM((2, count - 1, rows // TILE, TILE, half), jnp.bfloat16),
            pltpu.VMEM((2, rows // TILE, TILE, half), jnp.float32),
            pltpu.SemaphoreType.DMA((2, count - 1, rows // TILE)),
            pltpu.SemaphoreType.DMA((2, count - 1, rows // TILE)),
            pltpu.SemaphoreType.DMA((12,)),
            pltpu.SemaphoreType.DMA((12,)),
        ],
        compiler_params=pltpu.CompilerParams(
            collective_id=0, has_side_effects=True, vmem_limit_bytes=62 * 1024 * 1024
        ),
        cost_estimate=pl.CostEstimate(
            flops=4 * programs * depth * targets,
            bytes_accessed=2 * (2 * programs + targets) * depth + 4 * rows * targets,
            transcendentals=0,
        ),
    )(place.reshape(programs, 1), unit_rows, target_unit)


RING = 4
SLOT = (0, 2, 3, 1)


def wide_coords(w):
    return w // (2 * RING), (w // 2) % RING, w % 2


def wide_shift(x, axis_of_core, step):
    count = 2 * RING * RING
    perm = []
    for w in range(count):
        y, z, c = wide_coords(w)
        if axis_of_core[c] == "z":
            z = (z + step) % RING
        else:
            y = (y + step) % RING
        perm.append((w, (y * RING + z) * 2 + c))
    return lax.ppermute(x, "wide", perm)


def ring_gather(block, axis_of_core):
    half = block.shape[0] // 2
    from_left = wide_shift(block, axis_of_core, 1)
    from_right = wide_shift(block, axis_of_core, -1)
    far = jnp.concatenate(
        [
            wide_shift(from_left[:half], axis_of_core, 1),
            wide_shift(from_right[half:], axis_of_core, -1),
        ],
        axis=0,
    )
    return jnp.concatenate([block, from_left, from_right, far], axis=0)


def gathered_place(row_order, local):
    y, z, c = wide_coords(lax.axis_index("wide"))
    slot = jnp.asarray(SLOT, jnp.int32)
    owner = row_order // local
    oy, oz, oc = wide_coords(owner)
    dz, dy = (oz - z) % RING, (oy - y) % RING
    first_offset = jnp.where(oc == 0, dz, dy)
    second_offset = jnp.where(oc == 0, dy, dz)
    block = (oc != c) * (RING * RING) + slot[second_offset] * RING + slot[first_offset]
    return block * local + row_order % local


def shards(
    layer_input_rows,
    output_gradient_rows,
    adapter_up_weight,
    input_side_projection,
    rank_side_projection,
    lengths,
    program_output_index,
    targets,
):
    narrow_count = lax.axis_size("narrow")
    narrow_index = lax.axis_index("narrow")
    programs = lengths.shape[0]
    length = layer_input_rows.shape[0] // programs

    target_wide = targets.astype(jnp.float32)
    target_squares = jnp.sum(target_wide * target_wide, axis=1)
    target_squares = narrow_sum(
        target_squares, lambda dest: target_squares, narrow_count, narrow_index, jnp.float32
    )
    target_unit = normalize_rows(target_wide, target_squares)
    row_order = jnp.zeros_like(program_output_index).at[program_output_index].set(
        jnp.arange(program_output_index.shape[0], dtype=jnp.int32),
        mode="promise_in_bounds",
        unique_indices=True,
    )

    reduced_sums = jnp.dot(
        output_gradient_rows, adapter_up_weight, preferred_element_type=jnp.float32
    )
    out_part = jnp.dot(
        reduced_sums, rank_side_projection.astype(jnp.float32), precision=lax.Precision.HIGHEST
    )
    in_part = jnp.dot(layer_input_rows, input_side_projection, preferred_element_type=jnp.float32)
    quarter_cols = out_part.shape[1] // narrow_count

    def send_for(dest):
        quarter = lax.dynamic_slice_in_dim(out_part, dest * quarter_cols, quarter_cols, 1)
        return jnp.concatenate([quarter, in_part], axis=1)

    summed_parts = narrow_sum(send_for(narrow_index), send_for, narrow_count, narrow_index)
    summed_parts, target_unit, row_order = lax.optimization_barrier(
        (summed_parts, target_unit, row_order)
    )
    quarter = summed_parts[:, :quarter_cols]
    in_all = summed_parts[:, quarter_cols:]
    features = program_features(quarter, in_all, lengths, length)
    squares = jnp.sum(features * features, axis=1)
    squares = narrow_sum(squares, lambda dest: squares, narrow_count, narrow_index, jnp.float32)
    unit_rows = normalize_rows(features, squares)
    root_count = math.sqrt(float(targets.shape[1] * narrow_count))
    place = gathered_place(row_order, unit_rows.shape[0])
    return ring_scores(place, unit_rows, target_unit, narrow_count, root_count)


def solution(mesh):
    return jax.shard_map(
        shards,
        mesh=mesh,
        in_specs=(
            P("wide", "narrow"),
            P("wide", "narrow"),
            P("narrow", None),
            P("narrow", None),
            P(),
            P("wide"),
            P(),
            P("wide", "narrow"),
        ),
        out_specs=P("narrow", "wide"),
        check_vma=False,
    )
```

```python
import functools
import math

import jax
import jax.numpy as jnp
from jax import lax
from jax.experimental import pallas as pl
from jax.experimental.pallas import tpu as pltpu
from jax.sharding import PartitionSpec as P

MESH = pl.DeviceIdType.MESH

epsilon = 1e-06
TILE = 128


def program_features(out_side, in_side, lengths, length):
    programs = lengths.shape[0]
    positions = lax.broadcasted_iota(jnp.int32, (programs, length), 1)
    live_rows = (positions < lengths[:, None]).astype(jnp.float32)
    weighted = out_side.reshape(programs, length, -1) * live_rows[:, :, None]
    inputs = in_side.reshape(programs, length, -1)
    outer_sum = jnp.einsum("sla,slb->sab", weighted, inputs, precision=lax.Precision.HIGHEST)
    return outer_sum.reshape(programs, -1)


def normalize_rows(features, squares):
    return (features * lax.rsqrt(squares + epsilon)[:, None]).astype(jnp.bfloat16)


def narrow_sum(own, send_for, count, index, link_type=jnp.bfloat16):
    total = own
    for shift in range(1, count):
        perm = [(i, (i + shift) % count) for i in range(count)]
        piece = send_for((index + shift) % count).astype(link_type)
        total = total + lax.ppermute(piece, "narrow", perm).astype(jnp.float32)
    return total


def ring_kernel(count, root, dest_ref, rows_ref, t_ref, out_ref, gathered,
                ordered, send_buf, recv_buf, acc, send_sem, recv_sem, wide_send, wide_recv):
    me = lax.axis_index("narrow")
    right, left = lax.rem(me + 1, count), lax.rem(me + count - 1, count)
    rows = out_ref.shape[0]
    half = t_ref.shape[0] // 2
    tiles = rows // TILE
    local = rows_ref.shape[0]
    everyone = gathered.shape[0]

    wide = lax.axis_index("wide")
    y, z, core = wide // (2 * RING), (wide // 2) % RING, wide % 2

    def wide_peer(first_axis, step):
        along_z = (1 - core) if first_axis else core
        along_y = 1 - along_z
        return {"wide": (lax.rem(y + RING + step * along_y, RING) * RING
                         + lax.rem(z + RING + step * along_z, RING)) * 2 + core}

    partner = {"wide": wide + 1 - 2 * core}
    peers = [wide_peer(True, 1), wide_peer(True, -1), wide_peer(False, 1), wide_peer(False, -1), partner]

    barrier = pltpu.get_barrier_semaphore()
    for neighbour in (left, right):
        pl.semaphore_signal(barrier, inc=1, device_id={"narrow": neighbour}, device_id_type=MESH)
    for peer in peers:
        pl.semaphore_signal(barrier, inc=1, device_id=peer, device_id_type=MESH)
    pl.semaphore_wait(barrier, 2 + len(peers))

    def wide_copy(index, src, dst_start, size, peer):
        return pltpu.make_async_remote_copy(
            src_ref=src,
            dst_ref=gathered.at[pl.ds(dst_start, size)],
            send_sem=wide_send.at[index],
            recv_sem=wide_recv.at[index],
            device_id=peer,
            device_id_type=MESH,
        )

    def at(start, size):
        return gathered.at[pl.ds(start, size)]

    block, bundle = local, RING * local
    part_half, bundle_half = local // 2, bundle // 2
    plan = []
    plan.append(wide_copy(0, rows_ref, SLOT[RING - 1] * block, block, peers[0]))
    plan.append(wide_copy(1, rows_ref, SLOT[1] * block, block, peers[1]))
    gathered[0:block, :] = rows_ref[...]
    plan[0].start()
    plan[1].start()
    plan[0].wait_recv()
    plan.append(wide_copy(2, at(SLOT[RING - 1] * block, part_half), SLOT[2] * block, part_half, peers[0]))
    plan[2].start()
    plan[1].wait_recv()
    plan.append(wide_copy(3, at(SLOT[1] * block + part_half, part_half),
                          SLOT[2] * block + part_half, part_half, peers[1]))
    plan[3].start()
    plan[2].wait_recv()
    plan[3].wait_recv()
    plan.append(wide_copy(4, at(0, bundle), SLOT[RING - 1] * bundle, bundle, peers[2]))
    plan.append(wide_copy(5, at(0, bundle), SLOT[1] * bundle, bundle, peers[3]))
    plan.append(wide_copy(6, at(0, bundle), everyone // 2, bundle, partner))
    for copy in plan[4:7]:
        copy.start()
    plan[4].wait_recv()
    plan.append(wide_copy(7, at(SLOT[RING - 1] * bundle, bundle_half), SLOT[2] * bundle, bundle_half, peers[2]))
    plan.append(wide_copy(8, at(SLOT[RING - 1] * bundle, bundle), everyone // 2 + SLOT[RING - 1] * bundle,
                          bundle, partner))
    plan[7].start()
    plan[8].start()
    plan[5].wait_recv()
    plan.append(wide_copy(9, at(SLOT[1] * bundle + bundle_half, bundle_half),
                          SLOT[2] * bundle + bundle_half, bundle_half, peers[3]))
    plan.append(wide_copy(10, at(SLOT[1] * bundle, bundle), everyone // 2 + SLOT[1] * bundle,
                          bundle, partner))
    plan[9].start()
    plan[10].start()
    plan[7].wait_recv()
    plan[9].wait_recv()
    plan.append(wide_copy(11, at(SLOT[2] * bundle, bundle), everyone // 2 + SLOT[2] * bundle,
                          bundle, partner))
    plan[11].start()
    for index in (6, 8, 10, 11):
        plan[index].wait_recv()

    def order_rows(start):
        wanted = start + lax.broadcasted_iota(jnp.int32, (TILE, everyone), 0)
        pick = (dest_ref[...] == wanted).astype(jnp.bfloat16)
        picked = jnp.dot(pick, gathered[...], preferred_element_type=jnp.float32)
        ordered[pl.ds(start, TILE), :] = picked.astype(jnp.bfloat16)

    def partial_rows(start, direction, part):
        targets = t_ref[direction * half:(direction + 1) * half, :]
        acc[direction, part] = lax.dot_general(
            ordered[pl.ds(start, TILE), :], targets, (((1,), (1,)), ((), ())),
            preferred_element_type=jnp.float32,
        )

    def copy_of(direction, step, part):
        return pltpu.make_async_remote_copy(
            src_ref=send_buf.at[direction, step, part],
            dst_ref=recv_buf.at[direction, step, part],
            send_sem=send_sem.at[direction, step, part],
            recv_sem=recv_sem.at[direction, step, part],
            device_id={"narrow": right if direction == 0 else left},
            device_id_type=MESH,
        )

    built = set()
    for step in range(count - 1):
        offsets = ((2 * count - 1 - step) % count, (1 + step) % count)
        fresh = [offset not in built for offset in offsets]
        built.update(offsets)

        def body(part, carry, step=step, offsets=offsets, fresh=fresh):
            for direction in range(2):
                start = pl.multiple_of(lax.rem(me + offsets[direction], count) * rows + part * TILE, TILE)
                if fresh[direction] and not (direction == 1 and offsets[1] == offsets[0]):
                    order_rows(start)
                partial_rows(start, direction, part)
                if step == 0:
                    send_buf[direction, step, part] = acc[direction, part].astype(jnp.bfloat16)
                else:
                    copy_of(direction, step - 1, part).wait_recv()
                    send_buf[direction, step, part] = (
                        acc[direction, part] + recv_buf[direction, step - 1, part].astype(jnp.float32)
                    ).astype(jnp.bfloat16)
                copy_of(direction, step, part).start()
            return carry

        lax.fori_loop(0, tiles, body, 0)

    def last(part, carry):
        start = pl.multiple_of(me * rows + part * TILE, TILE)
        order_rows(start)
        for direction in range(2):
            partial_rows(start, direction, part)
            copy_of(direction, count - 2, part).wait_recv()
            out_ref[pl.ds(start - me * rows, TILE), direction * half:(direction + 1) * half] = (
                acc[direction, part] + recv_buf[direction, count - 2, part].astype(jnp.float32)
            ) * root
        return carry

    lax.fori_loop(0, tiles, last, 0)

    def drain(part, carry):
        for step in range(count - 1):
            for direction in range(2):
                copy_of(direction, step, part).wait_send()
        return carry

    lax.fori_loop(0, tiles, drain, 0)
    for copy in plan:
        copy.wait_send()


def ring_scores(dest, unit_rows, target_unit, count, root):
    programs = dest.shape[0]
    depth = unit_rows.shape[1]
    rows = programs // count
    targets = target_unit.shape[0]
    half = targets // 2
    return pl.pallas_call(
        functools.partial(ring_kernel, count, root),
        out_shape=jax.ShapeDtypeStruct((rows, targets), jnp.float32),
        in_specs=[pl.BlockSpec(memory_space=pltpu.VMEM)] * 3,
        out_specs=pl.BlockSpec(memory_space=pltpu.VMEM),
        scratch_shapes=[
            pltpu.VMEM((programs, depth), jnp.bfloat16),
            pltpu.VMEM((programs, depth), jnp.bfloat16),
            pltpu.VMEM((2, count - 1, rows // TILE, TILE, half), jnp.bfloat16),
            pltpu.VMEM((2, count - 1, rows // TILE, TILE, half), jnp.bfloat16),
            pltpu.VMEM((2, rows // TILE, TILE, half), jnp.float32),
            pltpu.SemaphoreType.DMA((2, count - 1, rows // TILE)),
            pltpu.SemaphoreType.DMA((2, count - 1, rows // TILE)),
            pltpu.SemaphoreType.DMA((12,)),
            pltpu.SemaphoreType.DMA((12,)),
        ],
        compiler_params=pltpu.CompilerParams(
            collective_id=0, has_side_effects=True, vmem_limit_bytes=62 * 1024 * 1024
        ),
        cost_estimate=pl.CostEstimate(
            flops=4 * programs * depth * targets,
            bytes_accessed=2 * (2 * programs + targets) * depth + 4 * rows * targets,
            transcendentals=0,
        ),
    )(dest.reshape(1, programs), unit_rows, target_unit)


RING = 4
SLOT = (0, 2, 3, 1)


def wide_coords(w):
    return w // (2 * RING), (w // 2) % RING, w % 2


def wide_shift(x, axis_of_core, step):
    count = 2 * RING * RING
    perm = []
    for w in range(count):
        y, z, c = wide_coords(w)
        if axis_of_core[c] == "z":
            z = (z + step) % RING
        else:
            y = (y + step) % RING
        perm.append((w, (y * RING + z) * 2 + c))
    return lax.ppermute(x, "wide", perm)


def ring_gather(block, axis_of_core):
    half = block.shape[0] // 2
    from_left = wide_shift(block, axis_of_core, 1)
    from_right = wide_shift(block, axis_of_core, -1)
    far = jnp.concatenate(
        [
            wide_shift(from_left[:half], axis_of_core, 1),
            wide_shift(from_right[half:], axis_of_core, -1),
        ],
        axis=0,
    )
    return jnp.concatenate([block, from_left, from_right, far], axis=0)


def gathered_dest(program_output_index, local):
    y, z, c = wide_coords(lax.axis_index("wide"))
    offset_of_slot = jnp.asarray([SLOT.index(k) for k in range(RING)], jnp.int32)
    position = jnp.arange(program_output_index.shape[0], dtype=jnp.int32)
    region, block, row = position // (RING * RING * local), (position // local) % (RING * RING), position % local
    first = offset_of_slot[block % RING]
    second = offset_of_slot[block // RING]
    oc = jnp.where(region == 0, c, 1 - c)
    oz = (z + jnp.where(oc == 0, first, second)) % RING
    oy = (y + jnp.where(oc == 0, second, first)) % RING
    program = ((oy * RING + oz) * 2 + oc) * local + row
    return program_output_index[program]


def shards(
    layer_input_rows,
    output_gradient_rows,
    adapter_up_weight,
    input_side_projection,
    rank_side_projection,
    lengths,
    program_output_index,
    targets,
):
    narrow_count = lax.axis_size("narrow")
    narrow_index = lax.axis_index("narrow")
    programs = lengths.shape[0]
    length = layer_input_rows.shape[0] // programs

    target_wide = targets.astype(jnp.float32)
    target_squares = jnp.sum(target_wide * target_wide, axis=1)
    target_squares = narrow_sum(
        target_squares, lambda dest: target_squares, narrow_count, narrow_index, jnp.float32
    )
    target_unit = normalize_rows(target_wide, target_squares)

    reduced_sums = jnp.dot(
        output_gradient_rows, adapter_up_weight, preferred_element_type=jnp.float32
    )
    out_part = jnp.dot(
        reduced_sums, rank_side_projection.astype(jnp.float32), precision=lax.Precision.HIGHEST
    )
    in_part = jnp.dot(layer_input_rows, input_side_projection, preferred_element_type=jnp.float32)
    quarter_cols = out_part.shape[1] // narrow_count

    def send_for(dest):
        quarter = lax.dynamic_slice_in_dim(out_part, dest * quarter_cols, quarter_cols, 1)
        return jnp.concatenate([quarter, in_part], axis=1)

    summed_parts = narrow_sum(send_for(narrow_index), send_for, narrow_count, narrow_index)
    summed_parts, target_unit = lax.optimization_barrier((summed_parts, target_unit))
    quarter = summed_parts[:, :quarter_cols]
    in_all = summed_parts[:, quarter_cols:]
    features = program_features(quarter, in_all, lengths, length)
    squares = jnp.sum(features * features, axis=1)
    squares = narrow_sum(squares, lambda dest: squares, narrow_count, narrow_index, jnp.float32)
    unit_rows = normalize_rows(features, squares)
    root_count = math.sqrt(float(targets.shape[1] * narrow_count))
    dest = gathered_dest(program_output_index, unit_rows.shape[0])
    return ring_scores(dest, unit_rows, target_unit, narrow_count, root_count)


def solution(mesh):
    return jax.shard_map(
        shards,
        mesh=mesh,
        in_specs=(
            P("wide", "narrow"),
            P("wide", "narrow"),
            P("narrow", None),
            P("narrow", None),
            P(),
            P("wide"),
            P(),
            P("wide", "narrow"),
        ),
        out_specs=P("narrow", "wide"),
        check_vma=False,
    )
```

```python
import functools
import math

import jax
import jax.numpy as jnp
from jax import lax
from jax.experimental import pallas as pl
from jax.experimental.pallas import tpu as pltpu
from jax.sharding import PartitionSpec as P

MESH = pl.DeviceIdType.MESH

epsilon = 1e-06
TILE = 128


def program_features(out_side, in_side, lengths, length):
    programs = lengths.shape[0]
    positions = lax.broadcasted_iota(jnp.int32, (programs, length), 1)
    live_rows = (positions < lengths[:, None]).astype(jnp.float32)
    weighted = out_side.reshape(programs, length, -1) * live_rows[:, :, None]
    inputs = in_side.reshape(programs, length, -1)
    outer_sum = jnp.einsum("sla,slb->sab", weighted, inputs, precision=lax.Precision.HIGHEST)
    return outer_sum.reshape(programs, -1)


def normalize_rows(features, squares):
    return (features * lax.rsqrt(squares + epsilon)[:, None]).astype(jnp.bfloat16)


def narrow_sum(own, send_for, count, index, link_type=jnp.bfloat16):
    total = own
    for shift in range(1, count):
        perm = [(i, (i + shift) % count) for i in range(count)]
        piece = send_for((index + shift) % count).astype(link_type)
        total = total + lax.ppermute(piece, "narrow", perm).astype(jnp.float32)
    return total


def ring_kernel(count, root, dest_ref, rows_ref, t_ref, out_ref, gathered,
                ordered, send_buf, recv_buf, acc, send_sem, recv_sem, wide_send, wide_recv):
    me = lax.axis_index("narrow")
    right, left = lax.rem(me + 1, count), lax.rem(me + count - 1, count)
    rows = out_ref.shape[0]
    half = t_ref.shape[0] // 2
    tiles = rows // TILE
    local = rows_ref.shape[0]
    everyone = gathered.shape[0]

    wide = lax.axis_index("wide")
    y, z, core = wide // (2 * RING), (wide // 2) % RING, wide % 2

    def wide_peer(first_axis, step):
        along_z = (1 - core) if first_axis else core
        along_y = 1 - along_z
        return {"wide": (lax.rem(y + RING + step * along_y, RING) * RING
                         + lax.rem(z + RING + step * along_z, RING)) * 2 + core}

    partner = {"wide": wide + 1 - 2 * core}
    peers = [wide_peer(True, 1), wide_peer(True, -1), wide_peer(False, 1), wide_peer(False, -1), partner]

    barrier = pltpu.get_barrier_semaphore()
    for neighbour in (left, right):
        pl.semaphore_signal(barrier, inc=1, device_id={"narrow": neighbour}, device_id_type=MESH)
    for peer in peers:
        pl.semaphore_signal(barrier, inc=1, device_id=peer, device_id_type=MESH)
    pl.semaphore_wait(barrier, 2 + len(peers))

    def wide_copy(index, src, dst_start, size, peer):
        return pltpu.make_async_remote_copy(
            src_ref=src,
            dst_ref=gathered.at[pl.ds(dst_start, size)],
            send_sem=wide_send.at[index],
            recv_sem=wide_recv.at[index],
            device_id=peer,
            device_id_type=MESH,
        )

    def at(start, size):
        return gathered.at[pl.ds(start, size)]

    block, bundle = local, RING * local
    part_half, bundle_half = local // 2, bundle // 2
    plan = []
    plan.append(wide_copy(0, rows_ref, SLOT[RING - 1] * block, block, peers[0]))
    plan.append(wide_copy(1, rows_ref, SLOT[1] * block, block, peers[1]))
    gathered[0:block, :] = rows_ref[...]
    plan[0].start()
    plan[1].start()
    plan[0].wait_recv()
    plan.append(wide_copy(2, at(SLOT[RING - 1] * block, part_half), SLOT[2] * block, part_half, peers[0]))
    plan[2].start()
    plan[1].wait_recv()
    plan.append(wide_copy(3, at(SLOT[1] * block + part_half, part_half),
                          SLOT[2] * block + part_half, part_half, peers[1]))
    plan[3].start()
    plan[2].wait_recv()
    plan[3].wait_recv()
    plan.append(wide_copy(4, at(0, bundle), SLOT[RING - 1] * bundle, bundle, peers[2]))
    plan.append(wide_copy(5, at(0, bundle), SLOT[1] * bundle, bundle, peers[3]))
    plan.append(wide_copy(6, at(0, bundle), everyone // 2, bundle, partner))
    for copy in plan[4:7]:
        copy.start()
    plan[4].wait_recv()
    plan.append(wide_copy(7, at(SLOT[RING - 1] * bundle, bundle_half), SLOT[2] * bundle, bundle_half, peers[2]))
    plan.append(wide_copy(8, at(SLOT[RING - 1] * bundle, bundle), everyone // 2 + SLOT[RING - 1] * bundle,
                          bundle, partner))
    plan[7].start()
    plan[8].start()
    plan[5].wait_recv()
    plan.append(wide_copy(9, at(SLOT[1] * bundle + bundle_half, bundle_half),
                          SLOT[2] * bundle + bundle_half, bundle_half, peers[3]))
    plan.append(wide_copy(10, at(SLOT[1] * bundle, bundle), everyone // 2 + SLOT[1] * bundle,
                          bundle, partner))
    plan[9].start()
    plan[10].start()
    plan[7].wait_recv()
    plan[9].wait_recv()
    plan.append(wide_copy(11, at(SLOT[2] * bundle, bundle), everyone // 2 + SLOT[2] * bundle,
                          bundle, partner))
    plan[11].start()
    for index in (6, 8, 10, 11):
        plan[index].wait_recv()

    def order_rows(start):
        wanted = start + lax.broadcasted_iota(jnp.int32, (TILE, everyone), 0)
        pick = (dest_ref[...] == wanted).astype(jnp.bfloat16)
        picked = jnp.dot(pick, gathered[...], preferred_element_type=jnp.float32)
        ordered[pl.ds(start, TILE), :] = picked.astype(jnp.bfloat16)

    def partial_rows(start, direction, part):
        targets = t_ref[direction * half:(direction + 1) * half, :]
        acc[direction, part] = lax.dot_general(
            ordered[pl.ds(start, TILE), :], targets, (((1,), (1,)), ((), ())),
            preferred_element_type=jnp.float32,
        )

    def copy_of(direction, step, part):
        return pltpu.make_async_remote_copy(
            src_ref=send_buf.at[direction, step, part],
            dst_ref=recv_buf.at[direction, step, part],
            send_sem=send_sem.at[direction, step, part],
            recv_sem=recv_sem.at[direction, step, part],
            device_id={"narrow": right if direction == 0 else left},
            device_id_type=MESH,
        )

    built = set()
    for step in range(count - 1):
        offsets = ((2 * count - 1 - step) % count, (1 + step) % count)
        fresh = [offset not in built for offset in offsets]
        built.update(offsets)

        def body(part, carry, step=step, offsets=offsets, fresh=fresh):
            for direction in range(2):
                start = pl.multiple_of(lax.rem(me + offsets[direction], count) * rows + part * TILE, TILE)
                if fresh[direction] and not (direction == 1 and offsets[1] == offsets[0]):
                    order_rows(start)
                partial_rows(start, direction, part)
                if step == 0:
                    send_buf[direction, step, part] = acc[direction, part].astype(jnp.bfloat16)
                else:
                    copy_of(direction, step - 1, part).wait_recv()
                    send_buf[direction, step, part] = (
                        acc[direction, part] + recv_buf[direction, step - 1, part].astype(jnp.float32)
                    ).astype(jnp.bfloat16)
                copy_of(direction, step, part).start()
            return carry

        lax.fori_loop(0, tiles, body, 0)

    def last(part, carry):
        start = pl.multiple_of(me * rows + part * TILE, TILE)
        order_rows(start)
        for direction in range(2):
            partial_rows(start, direction, part)
            copy_of(direction, count - 2, part).wait_recv()
            out_ref[pl.ds(start - me * rows, TILE), direction * half:(direction + 1) * half] = (
                acc[direction, part] + recv_buf[direction, count - 2, part].astype(jnp.float32)
            ) * root
        return carry

    lax.fori_loop(0, tiles, last, 0)

    def drain(part, carry):
        for step in range(count - 1):
            for direction in range(2):
                copy_of(direction, step, part).wait_send()
        return carry

    lax.fori_loop(0, tiles, drain, 0)
    for copy in plan:
        copy.wait_send()


def ring_scores(dest, unit_rows, target_unit, count, root):
    programs = dest.shape[0]
    depth = unit_rows.shape[1]
    rows = programs // count
    targets = target_unit.shape[0]
    half = targets // 2
    return pl.pallas_call(
        functools.partial(ring_kernel, count, root),
        out_shape=jax.ShapeDtypeStruct((rows, targets), jnp.float32),
        in_specs=[pl.BlockSpec(memory_space=pltpu.VMEM)] * 3,
        out_specs=pl.BlockSpec(memory_space=pltpu.VMEM),
        scratch_shapes=[
            pltpu.VMEM((programs, depth), jnp.bfloat16),
            pltpu.VMEM((programs, depth), jnp.bfloat16),
            pltpu.VMEM((2, count - 1, rows // TILE, TILE, half), jnp.bfloat16),
            pltpu.VMEM((2, count - 1, rows // TILE, TILE, half), jnp.bfloat16),
            pltpu.VMEM((2, rows // TILE, TILE, half), jnp.float32),
            pltpu.SemaphoreType.DMA((2, count - 1, rows // TILE)),
            pltpu.SemaphoreType.DMA((2, count - 1, rows // TILE)),
            pltpu.SemaphoreType.DMA((12,)),
            pltpu.SemaphoreType.DMA((12,)),
        ],
        compiler_params=pltpu.CompilerParams(
            collective_id=0, has_side_effects=True, vmem_limit_bytes=62 * 1024 * 1024
        ),
        cost_estimate=pl.CostEstimate(
            flops=4 * programs * depth * targets,
            bytes_accessed=2 * (2 * programs + targets) * depth + 4 * rows * targets,
            transcendentals=0,
        ),
    )(dest.reshape(1, programs), unit_rows, target_unit)


RING = 4
SLOT = (0, 2, 3, 1)


def wide_coords(w):
    return w // (2 * RING), (w // 2) % RING, w % 2


def wide_shift(x, axis_of_core, step):
    count = 2 * RING * RING
    perm = []
    for w in range(count):
        y, z, c = wide_coords(w)
        if axis_of_core[c] == "z":
            z = (z + step) % RING
        else:
            y = (y + step) % RING
        perm.append((w, (y * RING + z) * 2 + c))
    return lax.ppermute(x, "wide", perm)


def ring_gather(block, axis_of_core):
    half = block.shape[0] // 2
    from_left = wide_shift(block, axis_of_core, 1)
    from_right = wide_shift(block, axis_of_core, -1)
    far = jnp.concatenate(
        [
            wide_shift(from_left[:half], axis_of_core, 1),
            wide_shift(from_right[half:], axis_of_core, -1),
        ],
        axis=0,
    )
    return jnp.concatenate([block, from_left, from_right, far], axis=0)


def gathered_dest(program_output_index, local):
    y, z, c = wide_coords(lax.axis_index("wide"))
    offset_of_slot = jnp.asarray([SLOT.index(k) for k in range(RING)], jnp.int32)
    blocks = program_output_index.shape[0] // local
    position = jnp.arange(blocks, dtype=jnp.int32)
    region, block = position // (RING * RING), position % (RING * RING)
    first = offset_of_slot[block % RING]
    second = offset_of_slot[block // RING]
    oc = jnp.where(region == 0, c, 1 - c)
    oz = (z + jnp.where(oc == 0, first, second)) % RING
    oy = (y + jnp.where(oc == 0, second, first)) % RING
    owner = (oy * RING + oz) * 2 + oc
    pick = (owner[:, None] == jnp.arange(blocks, dtype=jnp.int32)[None, :]).astype(jnp.float32)
    by_owner = program_output_index.reshape(blocks, local).astype(jnp.float32)
    picked = jnp.dot(pick, by_owner, precision=lax.Precision.HIGHEST)
    return picked.astype(jnp.int32).reshape(-1)


def shards(
    layer_input_rows,
    output_gradient_rows,
    adapter_up_weight,
    input_side_projection,
    rank_side_projection,
    lengths,
    program_output_index,
    targets,
):
    narrow_count = lax.axis_size("narrow")
    narrow_index = lax.axis_index("narrow")
    programs = lengths.shape[0]
    length = layer_input_rows.shape[0] // programs

    target_wide = targets.astype(jnp.float32)
    target_squares = jnp.sum(target_wide * target_wide, axis=1)
    target_squares = narrow_sum(
        target_squares, lambda dest: target_squares, narrow_count, narrow_index, jnp.float32
    )
    target_unit = normalize_rows(target_wide, target_squares)

    reduced_sums = jnp.dot(
        output_gradient_rows, adapter_up_weight, preferred_element_type=jnp.float32
    )
    out_part = jnp.dot(
        reduced_sums, rank_side_projection.astype(jnp.float32), precision=lax.Precision.HIGHEST
    )
    in_part = jnp.dot(layer_input_rows, input_side_projection, preferred_element_type=jnp.float32)
    quarter_cols = out_part.shape[1] // narrow_count

    def send_for(dest):
        quarter = lax.dynamic_slice_in_dim(out_part, dest * quarter_cols, quarter_cols, 1)
        return jnp.concatenate([quarter, in_part], axis=1)

    summed_parts = narrow_sum(send_for(narrow_index), send_for, narrow_count, narrow_index)
    summed_parts, target_unit = lax.optimization_barrier((summed_parts, target_unit))
    quarter = summed_parts[:, :quarter_cols]
    in_all = summed_parts[:, quarter_cols:]
    features = program_features(quarter, in_all, lengths, length)
    squares = jnp.sum(features * features, axis=1)
    squares = narrow_sum(squares, lambda dest: squares, narrow_count, narrow_index, jnp.float32)
    unit_rows = normalize_rows(features, squares)
    root_count = math.sqrt(float(targets.shape[1] * narrow_count))
    dest = gathered_dest(program_output_index, unit_rows.shape[0])
    return ring_scores(dest, unit_rows, target_unit, narrow_count, root_count)


def solution(mesh):
    return jax.shard_map(
        shards,
        mesh=mesh,
        in_specs=(
            P("wide", "narrow"),
            P("wide", "narrow"),
            P("narrow", None),
            P("narrow", None),
            P(),
            P("wide"),
            P(),
            P("wide", "narrow"),
        ),
        out_specs=P("narrow", "wide"),
        check_vma=False,
    )
```

```python
import functools
import math

import jax
import jax.numpy as jnp
from jax import lax
from jax.experimental import pallas as pl
from jax.experimental.pallas import tpu as pltpu
from jax.sharding import PartitionSpec as P

MESH = pl.DeviceIdType.MESH

epsilon = 1e-06
TILE = 64


def program_features(out_side, in_side, lengths, length):
    programs = lengths.shape[0]
    positions = lax.broadcasted_iota(jnp.int32, (programs, length), 1)
    live_rows = (positions < lengths[:, None]).astype(jnp.float32)
    weighted = out_side.reshape(programs, length, -1) * live_rows[:, :, None]
    inputs = in_side.reshape(programs, length, -1)
    outer_sum = jnp.einsum("sla,slb->sab", weighted, inputs, precision=lax.Precision.HIGHEST)
    return outer_sum.reshape(programs, -1)


def normalize_rows(features, squares):
    return (features * lax.rsqrt(squares + epsilon)[:, None]).astype(jnp.bfloat16)


def narrow_sum(own, send_for, count, index, link_type=jnp.bfloat16):
    total = own
    for shift in range(1, count):
        perm = [(i, (i + shift) % count) for i in range(count)]
        piece = send_for((index + shift) % count).astype(link_type)
        total = total + lax.ppermute(piece, "narrow", perm).astype(jnp.float32)
    return total


def ring_kernel(count, root, dest_ref, rows_ref, t_ref, out_ref, gathered,
                ordered, send_buf, recv_buf, acc, send_sem, recv_sem, wide_send, wide_recv):
    me = lax.axis_index("narrow")
    right, left = lax.rem(me + 1, count), lax.rem(me + count - 1, count)
    rows = out_ref.shape[0]
    half = t_ref.shape[0] // 2
    tiles = rows // TILE
    local = rows_ref.shape[0]
    everyone = gathered.shape[0]

    wide = lax.axis_index("wide")
    y, z, core = wide // (2 * RING), (wide // 2) % RING, wide % 2

    def wide_peer(first_axis, step):
        along_z = (1 - core) if first_axis else core
        along_y = 1 - along_z
        return {"wide": (lax.rem(y + RING + step * along_y, RING) * RING
                         + lax.rem(z + RING + step * along_z, RING)) * 2 + core}

    partner = {"wide": wide + 1 - 2 * core}
    peers = [wide_peer(True, 1), wide_peer(True, -1), wide_peer(False, 1), wide_peer(False, -1), partner]

    barrier = pltpu.get_barrier_semaphore()
    for neighbour in (left, right):
        pl.semaphore_signal(barrier, inc=1, device_id={"narrow": neighbour}, device_id_type=MESH)
    for peer in peers:
        pl.semaphore_signal(barrier, inc=1, device_id=peer, device_id_type=MESH)
    pl.semaphore_wait(barrier, 2 + len(peers))

    def wide_copy(index, src, dst_start, size, peer):
        return pltpu.make_async_remote_copy(
            src_ref=src,
            dst_ref=gathered.at[pl.ds(dst_start, size)],
            send_sem=wide_send.at[index],
            recv_sem=wide_recv.at[index],
            device_id=peer,
            device_id_type=MESH,
        )

    def at(start, size):
        return gathered.at[pl.ds(start, size)]

    block, bundle = local, RING * local
    part_half, bundle_half = local // 2, bundle // 2
    plan = []
    plan.append(wide_copy(0, rows_ref, SLOT[RING - 1] * block, block, peers[0]))
    plan.append(wide_copy(1, rows_ref, SLOT[1] * block, block, peers[1]))
    gathered[0:block, :] = rows_ref[...]
    plan[0].start()
    plan[1].start()
    plan[0].wait_recv()
    plan.append(wide_copy(2, at(SLOT[RING - 1] * block, part_half), SLOT[2] * block, part_half, peers[0]))
    plan[2].start()
    plan[1].wait_recv()
    plan.append(wide_copy(3, at(SLOT[1] * block + part_half, part_half),
                          SLOT[2] * block + part_half, part_half, peers[1]))
    plan[3].start()
    plan[2].wait_recv()
    plan[3].wait_recv()
    plan.append(wide_copy(4, at(0, bundle), SLOT[RING - 1] * bundle, bundle, peers[2]))
    plan.append(wide_copy(5, at(0, bundle), SLOT[1] * bundle, bundle, peers[3]))
    plan.append(wide_copy(6, at(0, bundle), everyone // 2, bundle, partner))
    for copy in plan[4:7]:
        copy.start()
    plan[4].wait_recv()
    plan.append(wide_copy(7, at(SLOT[RING - 1] * bundle, bundle_half), SLOT[2] * bundle, bundle_half, peers[2]))
    plan.append(wide_copy(8, at(SLOT[RING - 1] * bundle, bundle), everyone // 2 + SLOT[RING - 1] * bundle,
                          bundle, partner))
    plan[7].start()
    plan[8].start()
    plan[5].wait_recv()
    plan.append(wide_copy(9, at(SLOT[1] * bundle + bundle_half, bundle_half),
                          SLOT[2] * bundle + bundle_half, bundle_half, peers[3]))
    plan.append(wide_copy(10, at(SLOT[1] * bundle, bundle), everyone // 2 + SLOT[1] * bundle,
                          bundle, partner))
    plan[9].start()
    plan[10].start()
    plan[7].wait_recv()
    plan[9].wait_recv()
    plan.append(wide_copy(11, at(SLOT[2] * bundle, bundle), everyone // 2 + SLOT[2] * bundle,
                          bundle, partner))
    plan[11].start()
    for index in (6, 8, 10, 11):
        plan[index].wait_recv()

    def order_rows(start):
        wanted = start + lax.broadcasted_iota(jnp.int32, (TILE, everyone), 0)
        pick = (dest_ref[...] == wanted).astype(jnp.bfloat16)
        picked = jnp.dot(pick, gathered[...], preferred_element_type=jnp.float32)
        ordered[pl.ds(start, TILE), :] = picked.astype(jnp.bfloat16)

    def partial_rows(start, direction, part):
        targets = t_ref[direction * half:(direction + 1) * half, :]
        acc[direction, part] = lax.dot_general(
            ordered[pl.ds(start, TILE), :], targets, (((1,), (1,)), ((), ())),
            preferred_element_type=jnp.float32,
        )

    def copy_of(direction, step, part):
        return pltpu.make_async_remote_copy(
            src_ref=send_buf.at[direction, step, part],
            dst_ref=recv_buf.at[direction, step, part],
            send_sem=send_sem.at[direction, step, part],
            recv_sem=recv_sem.at[direction, step, part],
            device_id={"narrow": right if direction == 0 else left},
            device_id_type=MESH,
        )

    built = set()
    for step in range(count - 1):
        offsets = ((2 * count - 1 - step) % count, (1 + step) % count)
        fresh = [offset not in built for offset in offsets]
        built.update(offsets)

        def body(part, carry, step=step, offsets=offsets, fresh=fresh):
            for direction in range(2):
                start = pl.multiple_of(lax.rem(me + offsets[direction], count) * rows + part * TILE, TILE)
                if fresh[direction] and not (direction == 1 and offsets[1] == offsets[0]):
                    order_rows(start)
                partial_rows(start, direction, part)
                if step == 0:
                    send_buf[direction, step, part] = acc[direction, part].astype(jnp.bfloat16)
                else:
                    copy_of(direction, step - 1, part).wait_recv()
                    send_buf[direction, step, part] = (
                        acc[direction, part] + recv_buf[direction, step - 1, part].astype(jnp.float32)
                    ).astype(jnp.bfloat16)
                copy_of(direction, step, part).start()
            return carry

        lax.fori_loop(0, tiles, body, 0)

    def last(part, carry):
        start = pl.multiple_of(me * rows + part * TILE, TILE)
        order_rows(start)
        for direction in range(2):
            partial_rows(start, direction, part)
            copy_of(direction, count - 2, part).wait_recv()
            out_ref[pl.ds(start - me * rows, TILE), direction * half:(direction + 1) * half] = (
                acc[direction, part] + recv_buf[direction, count - 2, part].astype(jnp.float32)
            ) * root
        return carry

    lax.fori_loop(0, tiles, last, 0)

    def drain(part, carry):
        for step in range(count - 1):
            for direction in range(2):
                copy_of(direction, step, part).wait_send()
        return carry

    lax.fori_loop(0, tiles, drain, 0)
    for copy in plan:
        copy.wait_send()


def ring_scores(dest, unit_rows, target_unit, count, root):
    programs = dest.shape[0]
    depth = unit_rows.shape[1]
    rows = programs // count
    targets = target_unit.shape[0]
    half = targets // 2
    return pl.pallas_call(
        functools.partial(ring_kernel, count, root),
        out_shape=jax.ShapeDtypeStruct((rows, targets), jnp.float32),
        in_specs=[pl.BlockSpec(memory_space=pltpu.VMEM)] * 3,
        out_specs=pl.BlockSpec(memory_space=pltpu.VMEM),
        scratch_shapes=[
            pltpu.VMEM((programs, depth), jnp.bfloat16),
            pltpu.VMEM((programs, depth), jnp.bfloat16),
            pltpu.VMEM((2, count - 1, rows // TILE, TILE, half), jnp.bfloat16),
            pltpu.VMEM((2, count - 1, rows // TILE, TILE, half), jnp.bfloat16),
            pltpu.VMEM((2, rows // TILE, TILE, half), jnp.float32),
            pltpu.SemaphoreType.DMA((2, count - 1, rows // TILE)),
            pltpu.SemaphoreType.DMA((2, count - 1, rows // TILE)),
            pltpu.SemaphoreType.DMA((12,)),
            pltpu.SemaphoreType.DMA((12,)),
        ],
        compiler_params=pltpu.CompilerParams(
            collective_id=0, has_side_effects=True, vmem_limit_bytes=62 * 1024 * 1024
        ),
        cost_estimate=pl.CostEstimate(
            flops=4 * programs * depth * targets,
            bytes_accessed=2 * (2 * programs + targets) * depth + 4 * rows * targets,
            transcendentals=0,
        ),
    )(dest.reshape(1, programs), unit_rows, target_unit)


RING = 4
SLOT = (0, 2, 3, 1)


def wide_coords(w):
    return w // (2 * RING), (w // 2) % RING, w % 2


def wide_shift(x, axis_of_core, step):
    count = 2 * RING * RING
    perm = []
    for w in range(count):
        y, z, c = wide_coords(w)
        if axis_of_core[c] == "z":
            z = (z + step) % RING
        else:
            y = (y + step) % RING
        perm.append((w, (y * RING + z) * 2 + c))
    return lax.ppermute(x, "wide", perm)


def ring_gather(block, axis_of_core):
    half = block.shape[0] // 2
    from_left = wide_shift(block, axis_of_core, 1)
    from_right = wide_shift(block, axis_of_core, -1)
    far = jnp.concatenate(
        [
            wide_shift(from_left[:half], axis_of_core, 1),
            wide_shift(from_right[half:], axis_of_core, -1),
        ],
        axis=0,
    )
    return jnp.concatenate([block, from_left, from_right, far], axis=0)


def gathered_dest(program_output_index, local):
    y, z, c = wide_coords(lax.axis_index("wide"))
    offset_of_slot = jnp.asarray([SLOT.index(k) for k in range(RING)], jnp.int32)
    blocks = program_output_index.shape[0] // local
    position = jnp.arange(blocks, dtype=jnp.int32)
    region, block = position // (RING * RING), position % (RING * RING)
    first = offset_of_slot[block % RING]
    second = offset_of_slot[block // RING]
    oc = jnp.where(region == 0, c, 1 - c)
    oz = (z + jnp.where(oc == 0, first, second)) % RING
    oy = (y + jnp.where(oc == 0, second, first)) % RING
    owner = (oy * RING + oz) * 2 + oc
    pick = (owner[:, None] == jnp.arange(blocks, dtype=jnp.int32)[None, :]).astype(jnp.float32)
    by_owner = program_output_index.reshape(blocks, local).astype(jnp.float32)
    picked = jnp.dot(pick, by_owner, precision=lax.Precision.HIGHEST)
    return picked.astype(jnp.int32).reshape(-1)


def shards(
    layer_input_rows,
    output_gradient_rows,
    adapter_up_weight,
    input_side_projection,
    rank_side_projection,
    lengths,
    program_output_index,
    targets,
):
    narrow_count = lax.axis_size("narrow")
    narrow_index = lax.axis_index("narrow")
    programs = lengths.shape[0]
    length = layer_input_rows.shape[0] // programs

    target_wide = targets.astype(jnp.float32)
    target_squares = jnp.sum(target_wide * target_wide, axis=1)
    target_squares = narrow_sum(
        target_squares, lambda dest: target_squares, narrow_count, narrow_index, jnp.float32
    )
    target_unit = normalize_rows(target_wide, target_squares)

    reduced_sums = jnp.dot(
        output_gradient_rows, adapter_up_weight, preferred_element_type=jnp.float32
    )
    out_part = jnp.dot(
        reduced_sums, rank_side_projection.astype(jnp.float32), precision=lax.Precision.HIGHEST
    )
    in_part = jnp.dot(layer_input_rows, input_side_projection, preferred_element_type=jnp.float32)
    quarter_cols = out_part.shape[1] // narrow_count

    def send_for(dest):
        quarter = lax.dynamic_slice_in_dim(out_part, dest * quarter_cols, quarter_cols, 1)
        return jnp.concatenate([quarter, in_part], axis=1)

    summed_parts = narrow_sum(send_for(narrow_index), send_for, narrow_count, narrow_index)
    summed_parts, target_unit = lax.optimization_barrier((summed_parts, target_unit))
    quarter = summed_parts[:, :quarter_cols]
    in_all = summed_parts[:, quarter_cols:]
    features = program_features(quarter, in_all, lengths, length)
    squares = jnp.sum(features * features, axis=1)
    squares = narrow_sum(squares, lambda dest: squares, narrow_count, narrow_index, jnp.float32)
    unit_rows = normalize_rows(features, squares)
    root_count = math.sqrt(float(targets.shape[1] * narrow_count))
    dest = gathered_dest(program_output_index, unit_rows.shape[0])
    return ring_scores(dest, unit_rows, target_unit, narrow_count, root_count)


def solution(mesh):
    return jax.shard_map(
        shards,
        mesh=mesh,
        in_specs=(
            P("wide", "narrow"),
            P("wide", "narrow"),
            P("narrow", None),
            P("narrow", None),
            P(),
            P("wide"),
            P(),
            P("wide", "narrow"),
        ),
        out_specs=P("narrow", "wide"),
        check_vma=False,
    )
```

```python
import functools
import math

import jax
import jax.numpy as jnp
from jax import lax
from jax.experimental import pallas as pl
from jax.experimental.pallas import tpu as pltpu
from jax.sharding import PartitionSpec as P

MESH = pl.DeviceIdType.MESH

epsilon = 1e-06
TILE = 128


def program_features(out_side, in_side, lengths, length):
    programs = lengths.shape[0]
    positions = lax.broadcasted_iota(jnp.int32, (programs, length), 1)
    live_rows = (positions < lengths[:, None]).astype(jnp.float32)
    weighted = out_side.reshape(programs, length, -1) * live_rows[:, :, None]
    inputs = in_side.reshape(programs, length, -1)
    outer_sum = jnp.einsum("sla,slb->sab", weighted, inputs, precision=lax.Precision.HIGHEST)
    return outer_sum.reshape(programs, -1)


def normalize_rows(features, squares):
    return (features * lax.rsqrt(squares + epsilon)[:, None]).astype(jnp.bfloat16)


def narrow_sum(own, send_for, count, index, link_type=jnp.bfloat16):
    total = own
    for shift in range(1, count):
        perm = [(i, (i + shift) % count) for i in range(count)]
        piece = send_for((index + shift) % count).astype(link_type)
        total = total + lax.ppermute(piece, "narrow", perm).astype(jnp.float32)
    return total


def ring_kernel(count, root, place_ref, feat_ref, t_ref, out_ref, gathered,
                ordered, send_buf, recv_buf, acc, send_sem, recv_sem, wide_send, wide_recv,
                rows_ref, sq_send, sq_recv, sq_send_sem, sq_recv_sem):
    me = lax.axis_index("narrow")
    right, left = lax.rem(me + 1, count), lax.rem(me + count - 1, count)
    rows = out_ref.shape[0]
    half = t_ref.shape[0] // 2
    tiles = rows // TILE
    local = feat_ref.shape[0]
    everyone = gathered.shape[0]

    wide = lax.axis_index("wide")
    y, z, core = wide // (2 * RING), (wide // 2) % RING, wide % 2

    def wide_peer(first_axis, step):
        along_z = (1 - core) if first_axis else core
        along_y = 1 - along_z
        return {"wide": (lax.rem(y + RING + step * along_y, RING) * RING
                         + lax.rem(z + RING + step * along_z, RING)) * 2 + core}

    partner = {"wide": wide + 1 - 2 * core}
    peers = [wide_peer(True, 1), wide_peer(True, -1), wide_peer(False, 1), wide_peer(False, -1), partner]

    narrow_peers = [lax.rem(me + shift, count) for shift in range(1, count)]
    barrier = pltpu.get_barrier_semaphore()
    for neighbour in narrow_peers:
        pl.semaphore_signal(barrier, inc=1, device_id={"narrow": neighbour}, device_id_type=MESH)
    for peer in peers:
        pl.semaphore_signal(barrier, inc=1, device_id=peer, device_id_type=MESH)
    pl.semaphore_wait(barrier, len(narrow_peers) + len(peers))

    features = feat_ref[...]
    sq_send[...] = jnp.broadcast_to(jnp.sum(features * features, axis=1, keepdims=True), sq_send.shape)
    squares_in = []
    for shift in range(1, count):
        squares_in.append(pltpu.make_async_remote_copy(
            src_ref=sq_send,
            dst_ref=sq_recv.at[shift - 1],
            send_sem=sq_send_sem.at[shift - 1],
            recv_sem=sq_recv_sem.at[shift - 1],
            device_id={"narrow": narrow_peers[shift - 1]},
            device_id_type=MESH,
        ))
        squares_in[-1].start()
    for copy in squares_in:
        copy.wait_recv()
    squares = sq_send[:, 0:1]
    for shift in range(1, count):
        squares = squares + sq_recv[shift - 1, :, 0:1]
    rows_ref[...] = (features * lax.rsqrt(squares + epsilon)).astype(jnp.bfloat16)
    for copy in squares_in:
        copy.wait_send()

    def wide_copy(index, src, dst_start, size, peer):
        return pltpu.make_async_remote_copy(
            src_ref=src,
            dst_ref=gathered.at[pl.ds(dst_start, size)],
            send_sem=wide_send.at[index],
            recv_sem=wide_recv.at[index],
            device_id=peer,
            device_id_type=MESH,
        )

    def at(start, size):
        return gathered.at[pl.ds(start, size)]

    block, bundle = local, RING * local
    part_half, bundle_half = local // 2, bundle // 2
    plan = []
    plan.append(wide_copy(0, rows_ref, SLOT[RING - 1] * block, block, peers[0]))
    plan.append(wide_copy(1, rows_ref, SLOT[1] * block, block, peers[1]))
    gathered[0:block, :] = rows_ref[...]
    plan[0].start()
    plan[1].start()
    plan[0].wait_recv()
    plan.append(wide_copy(2, at(SLOT[RING - 1] * block, part_half), SLOT[2] * block, part_half, peers[0]))
    plan[2].start()
    plan[1].wait_recv()
    plan.append(wide_copy(3, at(SLOT[1] * block + part_half, part_half),
                          SLOT[2] * block + part_half, part_half, peers[1]))
    plan[3].start()
    plan[2].wait_recv()
    plan[3].wait_recv()
    plan.append(wide_copy(4, at(0, bundle), SLOT[RING - 1] * bundle, bundle, peers[2]))
    plan.append(wide_copy(5, at(0, bundle), SLOT[1] * bundle, bundle, peers[3]))
    plan.append(wide_copy(6, at(0, bundle), everyone // 2, bundle, partner))
    for copy in plan[4:7]:
        copy.start()
    plan[4].wait_recv()
    plan.append(wide_copy(7, at(SLOT[RING - 1] * bundle, bundle_half), SLOT[2] * bundle, bundle_half, peers[2]))
    plan.append(wide_copy(8, at(SLOT[RING - 1] * bundle, bundle), everyone // 2 + SLOT[RING - 1] * bundle,
                          bundle, partner))
    plan[7].start()
    plan[8].start()
    plan[5].wait_recv()
    plan.append(wide_copy(9, at(SLOT[1] * bundle + bundle_half, bundle_half),
                          SLOT[2] * bundle + bundle_half, bundle_half, peers[3]))
    plan.append(wide_copy(10, at(SLOT[1] * bundle, bundle), everyone // 2 + SLOT[1] * bundle,
                          bundle, partner))
    plan[9].start()
    plan[10].start()
    plan[7].wait_recv()
    plan[9].wait_recv()
    plan.append(wide_copy(11, at(SLOT[2] * bundle, bundle), everyone // 2 + SLOT[2] * bundle,
                          bundle, partner))
    plan[11].start()
    for index in (6, 8, 10, 11):
        plan[index].wait_recv()

    def order_rows(start):
        wanted = place_ref[pl.ds(start, TILE), :]
        columns = lax.broadcasted_iota(jnp.int32, (TILE, everyone), 1)
        pick = (wanted == columns).astype(jnp.bfloat16)
        picked = jnp.dot(pick, gathered[...], preferred_element_type=jnp.float32)
        ordered[pl.ds(start, TILE), :] = picked.astype(jnp.bfloat16)

    def partial_rows(start, direction, part):
        targets = t_ref[direction * half:(direction + 1) * half, :]
        acc[direction, part] = lax.dot_general(
            ordered[pl.ds(start, TILE), :], targets, (((1,), (1,)), ((), ())),
            preferred_element_type=jnp.float32,
        )

    def copy_of(direction, step, part):
        return pltpu.make_async_remote_copy(
            src_ref=send_buf.at[direction, step, part],
            dst_ref=recv_buf.at[direction, step, part],
            send_sem=send_sem.at[direction, step, part],
            recv_sem=recv_sem.at[direction, step, part],
            device_id={"narrow": right if direction == 0 else left},
            device_id_type=MESH,
        )

    built = set()
    for step in range(count - 1):
        offsets = ((2 * count - 1 - step) % count, (1 + step) % count)
        fresh = [offset not in built for offset in offsets]
        built.update(offsets)

        def body(part, carry, step=step, offsets=offsets, fresh=fresh):
            for direction in range(2):
                start = pl.multiple_of(lax.rem(me + offsets[direction], count) * rows + part * TILE, TILE)
                if fresh[direction] and not (direction == 1 and offsets[1] == offsets[0]):
                    order_rows(start)
                partial_rows(start, direction, part)
                if step == 0:
                    send_buf[direction, step, part] = acc[direction, part].astype(jnp.bfloat16)
                else:
                    copy_of(direction, step - 1, part).wait_recv()
                    send_buf[direction, step, part] = (
                        acc[direction, part] + recv_buf[direction, step - 1, part].astype(jnp.float32)
                    ).astype(jnp.bfloat16)
                copy_of(direction, step, part).start()
            return carry

        lax.fori_loop(0, tiles, body, 0)

    def last(part, carry):
        start = pl.multiple_of(me * rows + part * TILE, TILE)
        order_rows(start)
        for direction in range(2):
            partial_rows(start, direction, part)
            copy_of(direction, count - 2, part).wait_recv()
            out_ref[pl.ds(start - me * rows, TILE), direction * half:(direction + 1) * half] = (
                acc[direction, part] + recv_buf[direction, count - 2, part].astype(jnp.float32)
            ) * root
        return carry

    lax.fori_loop(0, tiles, last, 0)

    def drain(part, carry):
        for step in range(count - 1):
            for direction in range(2):
                copy_of(direction, step, part).wait_send()
        return carry

    lax.fori_loop(0, tiles, drain, 0)
    for copy in plan:
        copy.wait_send()


def ring_scores(place, features, target_unit, count, root):
    programs = place.shape[0]
    local, depth = features.shape
    rows = programs // count
    targets = target_unit.shape[0]
    half = targets // 2
    return pl.pallas_call(
        functools.partial(ring_kernel, count, root),
        out_shape=jax.ShapeDtypeStruct((rows, targets), jnp.float32),
        in_specs=[pl.BlockSpec(memory_space=pltpu.VMEM)] * 3,
        out_specs=pl.BlockSpec(memory_space=pltpu.VMEM),
        scratch_shapes=[
            pltpu.VMEM((programs, depth), jnp.bfloat16),
            pltpu.VMEM((programs, depth), jnp.bfloat16),
            pltpu.VMEM((2, count - 1, rows // TILE, TILE, half), jnp.bfloat16),
            pltpu.VMEM((2, count - 1, rows // TILE, TILE, half), jnp.bfloat16),
            pltpu.VMEM((2, rows // TILE, TILE, half), jnp.float32),
            pltpu.SemaphoreType.DMA((2, count - 1, rows // TILE)),
            pltpu.SemaphoreType.DMA((2, count - 1, rows // TILE)),
            pltpu.SemaphoreType.DMA((12,)),
            pltpu.SemaphoreType.DMA((12,)),
            pltpu.VMEM((local, depth), jnp.bfloat16),
            pltpu.VMEM((local, 128), jnp.float32),
            pltpu.VMEM((count - 1, local, 128), jnp.float32),
            pltpu.SemaphoreType.DMA((count - 1,)),
            pltpu.SemaphoreType.DMA((count - 1,)),
        ],
        compiler_params=pltpu.CompilerParams(
            collective_id=0, has_side_effects=True, vmem_limit_bytes=62 * 1024 * 1024
        ),
        cost_estimate=pl.CostEstimate(
            flops=4 * programs * depth * targets,
            bytes_accessed=2 * (2 * programs + targets) * depth + 4 * rows * targets,
            transcendentals=0,
        ),
    )(place.reshape(programs, 1), features, target_unit)


RING = 4
SLOT = (0, 2, 3, 1)


def wide_coords(w):
    return w // (2 * RING), (w // 2) % RING, w % 2


def wide_shift(x, axis_of_core, step):
    count = 2 * RING * RING
    perm = []
    for w in range(count):
        y, z, c = wide_coords(w)
        if axis_of_core[c] == "z":
            z = (z + step) % RING
        else:
            y = (y + step) % RING
        perm.append((w, (y * RING + z) * 2 + c))
    return lax.ppermute(x, "wide", perm)


def ring_gather(block, axis_of_core):
    half = block.shape[0] // 2
    from_left = wide_shift(block, axis_of_core, 1)
    from_right = wide_shift(block, axis_of_core, -1)
    far = jnp.concatenate(
        [
            wide_shift(from_left[:half], axis_of_core, 1),
            wide_shift(from_right[half:], axis_of_core, -1),
        ],
        axis=0,
    )
    return jnp.concatenate([block, from_left, from_right, far], axis=0)


def gathered_place(row_order, local):
    y, z, c = wide_coords(lax.axis_index("wide"))
    slot = jnp.asarray(SLOT, jnp.int32)
    owner = row_order // local
    oy, oz, oc = wide_coords(owner)
    dz, dy = (oz - z) % RING, (oy - y) % RING
    first_offset = jnp.where(oc == 0, dz, dy)
    second_offset = jnp.where(oc == 0, dy, dz)
    block = (oc != c) * (RING * RING) + slot[second_offset] * RING + slot[first_offset]
    return block * local + row_order % local


def shards(
    layer_input_rows,
    output_gradient_rows,
    adapter_up_weight,
    input_side_projection,
    rank_side_projection,
    lengths,
    program_output_index,
    targets,
):
    narrow_count = lax.axis_size("narrow")
    narrow_index = lax.axis_index("narrow")
    programs = lengths.shape[0]
    length = layer_input_rows.shape[0] // programs

    target_wide = targets.astype(jnp.float32)
    target_squares = jnp.sum(target_wide * target_wide, axis=1)
    target_squares = narrow_sum(
        target_squares, lambda dest: target_squares, narrow_count, narrow_index, jnp.float32
    )
    target_unit = normalize_rows(target_wide, target_squares)
    row_order = jnp.zeros_like(program_output_index).at[program_output_index].set(
        jnp.arange(program_output_index.shape[0], dtype=jnp.int32),
        mode="promise_in_bounds",
        unique_indices=True,
    )

    reduced_sums = jnp.dot(
        output_gradient_rows, adapter_up_weight, preferred_element_type=jnp.float32
    )
    out_part = jnp.dot(
        reduced_sums, rank_side_projection.astype(jnp.float32), precision=lax.Precision.HIGHEST
    )
    in_part = jnp.dot(layer_input_rows, input_side_projection, preferred_element_type=jnp.float32)
    quarter_cols = out_part.shape[1] // narrow_count

    def send_for(dest):
        quarter = lax.dynamic_slice_in_dim(out_part, dest * quarter_cols, quarter_cols, 1)
        return jnp.concatenate([quarter, in_part], axis=1)

    summed_parts = narrow_sum(send_for(narrow_index), send_for, narrow_count, narrow_index)
    summed_parts, target_unit, row_order = lax.optimization_barrier(
        (summed_parts, target_unit, row_order)
    )
    quarter = summed_parts[:, :quarter_cols]
    in_all = summed_parts[:, quarter_cols:]
    features = program_features(quarter, in_all, lengths, length)
    root_count = math.sqrt(float(targets.shape[1] * narrow_count))
    place = gathered_place(row_order, features.shape[0])
    return ring_scores(place, features, target_unit, narrow_count, root_count)


def solution(mesh):
    return jax.shard_map(
        shards,
        mesh=mesh,
        in_specs=(
            P("wide", "narrow"),
            P("wide", "narrow"),
            P("narrow", None),
            P("narrow", None),
            P(),
            P("wide"),
            P(),
            P("wide", "narrow"),
        ),
        out_specs=P("narrow", "wide"),
        check_vma=False,
    )
```

```python
import functools
import math

import jax
import jax.numpy as jnp
from jax import lax
from jax.experimental import pallas as pl
from jax.experimental.pallas import tpu as pltpu
from jax.sharding import PartitionSpec as P

MESH = pl.DeviceIdType.MESH

epsilon = 1e-06
TILE = 128


def program_features(out_side, in_side, lengths, length):
    programs = lengths.shape[0]
    positions = lax.broadcasted_iota(jnp.int32, (programs, length), 1)
    live_rows = (positions < lengths[:, None]).astype(jnp.float32)
    weighted = out_side.reshape(programs, length, -1) * live_rows[:, :, None]
    inputs = in_side.reshape(programs, length, -1)
    outer_sum = jnp.einsum("sla,slb->sab", weighted, inputs, precision=lax.Precision.HIGHEST)
    return outer_sum.reshape(programs, -1)


def normalize_rows(features, squares):
    return (features * lax.rsqrt(squares + epsilon)[:, None]).astype(jnp.bfloat16)


def narrow_sum(own, send_for, count, index, link_type=jnp.bfloat16):
    total = own
    for shift in range(1, count):
        perm = [(i, (i + shift) % count) for i in range(count)]
        piece = send_for((index + shift) % count).astype(link_type)
        total = total + lax.ppermute(piece, "narrow", perm).astype(jnp.float32)
    return total


def ring_kernel(count, root, dest_ref, feat_ref, t_ref, out_ref, gathered,
                ordered, send_buf, recv_buf, acc, send_sem, recv_sem, wide_send, wide_recv,
                rows_ref, sq_send, sq_recv, sq_send_sem, sq_recv_sem):
    me = lax.axis_index("narrow")
    right, left = lax.rem(me + 1, count), lax.rem(me + count - 1, count)
    rows = out_ref.shape[0]
    half = t_ref.shape[0] // 2
    tiles = rows // TILE
    local = feat_ref.shape[0]
    everyone = gathered.shape[0]

    wide = lax.axis_index("wide")
    y, z, core = wide // (2 * RING), (wide // 2) % RING, wide % 2

    def wide_peer(first_axis, step):
        along_z = (1 - core) if first_axis else core
        along_y = 1 - along_z
        return {"wide": (lax.rem(y + RING + step * along_y, RING) * RING
                         + lax.rem(z + RING + step * along_z, RING)) * 2 + core}

    partner = {"wide": wide + 1 - 2 * core}
    peers = [wide_peer(True, 1), wide_peer(True, -1), wide_peer(False, 1), wide_peer(False, -1), partner]

    narrow_peers = [lax.rem(me + shift, count) for shift in range(1, count)]
    barrier = pltpu.get_barrier_semaphore()
    for neighbour in narrow_peers:
        pl.semaphore_signal(barrier, inc=1, device_id={"narrow": neighbour}, device_id_type=MESH)
    for peer in peers:
        pl.semaphore_signal(barrier, inc=1, device_id=peer, device_id_type=MESH)
    features = feat_ref[...]
    sq_send[...] = jnp.broadcast_to(jnp.sum(features * features, axis=1, keepdims=True), sq_send.shape)
    pl.semaphore_wait(barrier, len(narrow_peers) + len(peers))
    squares_in = []
    for shift in range(1, count):
        squares_in.append(pltpu.make_async_remote_copy(
            src_ref=sq_send,
            dst_ref=sq_recv.at[shift - 1],
            send_sem=sq_send_sem.at[shift - 1],
            recv_sem=sq_recv_sem.at[shift - 1],
            device_id={"narrow": narrow_peers[shift - 1]},
            device_id_type=MESH,
        ))
        squares_in[-1].start()
    for copy in squares_in:
        copy.wait_recv()
    squares = sq_send[:, 0:1]
    for shift in range(1, count):
        squares = squares + sq_recv[shift - 1, :, 0:1]
    rows_ref[...] = (features * lax.rsqrt(squares + epsilon)).astype(jnp.bfloat16)
    for copy in squares_in:
        copy.wait_send()

    def wide_copy(index, src, dst_start, size, peer):
        return pltpu.make_async_remote_copy(
            src_ref=src,
            dst_ref=gathered.at[pl.ds(dst_start, size)],
            send_sem=wide_send.at[index],
            recv_sem=wide_recv.at[index],
            device_id=peer,
            device_id_type=MESH,
        )

    def at(start, size):
        return gathered.at[pl.ds(start, size)]

    block, bundle = local, RING * local
    part_half, bundle_half = local // 2, bundle // 2
    plan = []
    plan.append(wide_copy(0, rows_ref, SLOT[RING - 1] * block, block, peers[0]))
    plan.append(wide_copy(1, rows_ref, SLOT[1] * block, block, peers[1]))
    gathered[0:block, :] = rows_ref[...]
    plan[0].start()
    plan[1].start()
    plan[0].wait_recv()
    plan.append(wide_copy(2, at(SLOT[RING - 1] * block, part_half), SLOT[2] * block, part_half, peers[0]))
    plan[2].start()
    plan[1].wait_recv()
    plan.append(wide_copy(3, at(SLOT[1] * block + part_half, part_half),
                          SLOT[2] * block + part_half, part_half, peers[1]))
    plan[3].start()
    plan[2].wait_recv()
    plan[3].wait_recv()
    plan.append(wide_copy(4, at(0, bundle), SLOT[RING - 1] * bundle, bundle, peers[2]))
    plan.append(wide_copy(5, at(0, bundle), SLOT[1] * bundle, bundle, peers[3]))
    plan.append(wide_copy(6, at(0, bundle), everyone // 2, bundle, partner))
    for copy in plan[4:7]:
        copy.start()
    plan[4].wait_recv()
    plan.append(wide_copy(7, at(SLOT[RING - 1] * bundle, bundle_half), SLOT[2] * bundle, bundle_half, peers[2]))
    plan.append(wide_copy(8, at(SLOT[RING - 1] * bundle, bundle), everyone // 2 + SLOT[RING - 1] * bundle,
                          bundle, partner))
    plan[7].start()
    plan[8].start()
    plan[5].wait_recv()
    plan.append(wide_copy(9, at(SLOT[1] * bundle + bundle_half, bundle_half),
                          SLOT[2] * bundle + bundle_half, bundle_half, peers[3]))
    plan.append(wide_copy(10, at(SLOT[1] * bundle, bundle), everyone // 2 + SLOT[1] * bundle,
                          bundle, partner))
    plan[9].start()
    plan[10].start()
    plan[7].wait_recv()
    plan[9].wait_recv()
    plan.append(wide_copy(11, at(SLOT[2] * bundle, bundle), everyone // 2 + SLOT[2] * bundle,
                          bundle, partner))
    plan[11].start()
    for index in (6, 8, 10, 11):
        plan[index].wait_recv()

    def order_rows(start):
        wanted = start + lax.broadcasted_iota(jnp.int32, (TILE, everyone), 0)
        pick = (dest_ref[...] == wanted).astype(jnp.bfloat16)
        picked = jnp.dot(pick, gathered[...], preferred_element_type=jnp.float32)
        ordered[pl.ds(start, TILE), :] = picked.astype(jnp.bfloat16)

    def partial_rows(start, direction, part):
        targets = t_ref[direction * half:(direction + 1) * half, :]
        acc[direction, part] = lax.dot_general(
            ordered[pl.ds(start, TILE), :], targets, (((1,), (1,)), ((), ())),
            preferred_element_type=jnp.float32,
        )

    def copy_of(direction, step, part):
        return pltpu.make_async_remote_copy(
            src_ref=send_buf.at[direction, step, part],
            dst_ref=recv_buf.at[direction, step, part],
            send_sem=send_sem.at[direction, step, part],
            recv_sem=recv_sem.at[direction, step, part],
            device_id={"narrow": right if direction == 0 else left},
            device_id_type=MESH,
        )

    built = set()
    for step in range(count - 1):
        offsets = ((2 * count - 1 - step) % count, (1 + step) % count)
        fresh = [offset not in built for offset in offsets]
        built.update(offsets)

        def body(part, carry, step=step, offsets=offsets, fresh=fresh):
            for direction in range(2):
                start = pl.multiple_of(lax.rem(me + offsets[direction], count) * rows + part * TILE, TILE)
                if fresh[direction] and not (direction == 1 and offsets[1] == offsets[0]):
                    order_rows(start)
                partial_rows(start, direction, part)
                if step == 0:
                    send_buf[direction, step, part] = acc[direction, part].astype(jnp.bfloat16)
                else:
                    copy_of(direction, step - 1, part).wait_recv()
                    send_buf[direction, step, part] = (
                        acc[direction, part] + recv_buf[direction, step - 1, part].astype(jnp.float32)
                    ).astype(jnp.bfloat16)
                copy_of(direction, step, part).start()
            return carry

        lax.fori_loop(0, tiles, body, 0)

    def last(part, carry):
        start = pl.multiple_of(me * rows + part * TILE, TILE)
        order_rows(start)
        for direction in range(2):
            partial_rows(start, direction, part)
            copy_of(direction, count - 2, part).wait_recv()
            out_ref[pl.ds(start - me * rows, TILE), direction * half:(direction + 1) * half] = (
                acc[direction, part] + recv_buf[direction, count - 2, part].astype(jnp.float32)
            ) * root
        return carry

    lax.fori_loop(0, tiles, last, 0)

    def drain(part, carry):
        for step in range(count - 1):
            for direction in range(2):
                copy_of(direction, step, part).wait_send()
        return carry

    lax.fori_loop(0, tiles, drain, 0)
    for copy in plan:
        copy.wait_send()


def ring_scores(dest, features, target_unit, count, root):
    programs = dest.shape[0]
    local, depth = features.shape
    rows = programs // count
    targets = target_unit.shape[0]
    half = targets // 2
    return pl.pallas_call(
        functools.partial(ring_kernel, count, root),
        out_shape=jax.ShapeDtypeStruct((rows, targets), jnp.float32),
        in_specs=[pl.BlockSpec(memory_space=pltpu.VMEM)] * 3,
        out_specs=pl.BlockSpec(memory_space=pltpu.VMEM),
        scratch_shapes=[
            pltpu.VMEM((programs, depth), jnp.bfloat16),
            pltpu.VMEM((programs, depth), jnp.bfloat16),
            pltpu.VMEM((2, count - 1, rows // TILE, TILE, half), jnp.bfloat16),
            pltpu.VMEM((2, count - 1, rows // TILE, TILE, half), jnp.bfloat16),
            pltpu.VMEM((2, rows // TILE, TILE, half), jnp.float32),
            pltpu.SemaphoreType.DMA((2, count - 1, rows // TILE)),
            pltpu.SemaphoreType.DMA((2, count - 1, rows // TILE)),
            pltpu.SemaphoreType.DMA((12,)),
            pltpu.SemaphoreType.DMA((12,)),
            pltpu.VMEM((local, depth), jnp.bfloat16),
            pltpu.VMEM((local, 128), jnp.float32),
            pltpu.VMEM((count - 1, local, 128), jnp.float32),
            pltpu.SemaphoreType.DMA((count - 1,)),
            pltpu.SemaphoreType.DMA((count - 1,)),
        ],
        compiler_params=pltpu.CompilerParams(
            collective_id=0, has_side_effects=True, vmem_limit_bytes=62 * 1024 * 1024
        ),
        cost_estimate=pl.CostEstimate(
            flops=4 * programs * depth * targets,
            bytes_accessed=2 * (2 * programs + targets) * depth + 4 * rows * targets,
            transcendentals=0,
        ),
    )(dest.reshape(1, programs), features, target_unit)


RING = 4
SLOT = (0, 2, 3, 1)


def wide_coords(w):
    return w // (2 * RING), (w // 2) % RING, w % 2


def wide_shift(x, axis_of_core, step):
    count = 2 * RING * RING
    perm = []
    for w in range(count):
        y, z, c = wide_coords(w)
        if axis_of_core[c] == "z":
            z = (z + step) % RING
        else:
            y = (y + step) % RING
        perm.append((w, (y * RING + z) * 2 + c))
    return lax.ppermute(x, "wide", perm)


def ring_gather(block, axis_of_core):
    half = block.shape[0] // 2
    from_left = wide_shift(block, axis_of_core, 1)
    from_right = wide_shift(block, axis_of_core, -1)
    far = jnp.concatenate(
        [
            wide_shift(from_left[:half], axis_of_core, 1),
            wide_shift(from_right[half:], axis_of_core, -1),
        ],
        axis=0,
    )
    return jnp.concatenate([block, from_left, from_right, far], axis=0)


def gathered_dest(program_output_index, local):
    y, z, c = wide_coords(lax.axis_index("wide"))
    offset_of_slot = jnp.asarray([SLOT.index(k) for k in range(RING)], jnp.int32)
    blocks = program_output_index.shape[0] // local
    position = jnp.arange(blocks, dtype=jnp.int32)
    region, block = position // (RING * RING), position % (RING * RING)
    first = offset_of_slot[block % RING]
    second = offset_of_slot[block // RING]
    oc = jnp.where(region == 0, c, 1 - c)
    oz = (z + jnp.where(oc == 0, first, second)) % RING
    oy = (y + jnp.where(oc == 0, second, first)) % RING
    owner = (oy * RING + oz) * 2 + oc
    pick = (owner[:, None] == jnp.arange(blocks, dtype=jnp.int32)[None, :]).astype(jnp.float32)
    by_owner = program_output_index.reshape(blocks, local).astype(jnp.float32)
    picked = jnp.dot(pick, by_owner, precision=lax.Precision.HIGHEST)
    return picked.astype(jnp.int32).reshape(-1)


def shards(
    layer_input_rows,
    output_gradient_rows,
    adapter_up_weight,
    input_side_projection,
    rank_side_projection,
    lengths,
    program_output_index,
    targets,
):
    narrow_count = lax.axis_size("narrow")
    narrow_index = lax.axis_index("narrow")
    programs = lengths.shape[0]
    length = layer_input_rows.shape[0] // programs

    target_wide = targets.astype(jnp.float32)
    target_squares = jnp.sum(target_wide * target_wide, axis=1)
    target_squares = narrow_sum(
        target_squares, lambda dest: target_squares, narrow_count, narrow_index, jnp.float32
    )
    target_unit = normalize_rows(target_wide, target_squares)

    reduced_sums = jnp.dot(
        output_gradient_rows, adapter_up_weight, preferred_element_type=jnp.float32
    )
    out_part = jnp.dot(
        reduced_sums, rank_side_projection.astype(jnp.float32), precision=lax.Precision.HIGHEST
    )
    in_part = jnp.dot(layer_input_rows, input_side_projection, preferred_element_type=jnp.float32)
    quarter_cols = out_part.shape[1] // narrow_count

    def send_for(dest):
        quarter = lax.dynamic_slice_in_dim(out_part, dest * quarter_cols, quarter_cols, 1)
        return jnp.concatenate([quarter, in_part], axis=1)

    summed_parts = narrow_sum(send_for(narrow_index), send_for, narrow_count, narrow_index)
    summed_parts, target_unit = lax.optimization_barrier((summed_parts, target_unit))
    quarter = summed_parts[:, :quarter_cols]
    in_all = summed_parts[:, quarter_cols:]
    features = program_features(quarter, in_all, lengths, length)
    root_count = math.sqrt(float(targets.shape[1] * narrow_count))
    dest = gathered_dest(program_output_index, features.shape[0])
    return ring_scores(dest, features, target_unit, narrow_count, root_count)


def solution(mesh):
    return jax.shard_map(
        shards,
        mesh=mesh,
        in_specs=(
            P("wide", "narrow"),
            P("wide", "narrow"),
            P("narrow", None),
            P("narrow", None),
            P(),
            P("wide"),
            P(),
            P("wide", "narrow"),
        ),
        out_specs=P("narrow", "wide"),
        check_vma=False,
    )
```
